256 devices in a mesh: row: 4 (over x), tile: 64 (over z, y, core).
Axes of the slice: x: 4, y: 4, z: 8, core: 2. Of those that a mesh axis runs over, the one named last changes fastest.
Arguments:
- row_points: float32 [3, 16384], replicated, may hold values from 0 to 6, as said below
- source_points: float32 [3, 262144], P(None, 'tile'), may hold values from -2.5 to 6, as said below
- sketch: bfloat16 [262144, 128], P('tile'), may hold values from -6 to 6
- admissible: int32 [4, 2048], P('row', 'tile'), may hold values from 0 to 1, as said below
Outputs:
- basis: float32 [16384, 128], P(('row', 'tile'))
- projected: bfloat16 [4, 128, 262144], P('row', None, 'tile')
The draws below stay inside these ranges and needn't reach their ends.
Inputs may be any that keep to these rules, and one draw needn't show every extreme that they name: In every block row, the 32 panels of some index of tile are all admissible; how many panels of an index of tile are admissible varies widely. `row_points`: the first two coordinates lie in 0 to 6 and the third in 0 to 0.25. `source_points`: the first two coordinates lie in 0 to 6 and the third in -2.5 to -0.5.
All inputs are finite; a program needn't handle non-finite values.
Results may differ from the reference program's by a relative error of at most 0.0055.
Values may be sent and summed in bfloat16 or wider, within the bound.
A program may use at most 64 MiB of HBM per device.

```python
import math
import jax
import jax.numpy as jnp
from jax import lax

CS = 4096
K = 128
PW = 128
PAN_DEV = 32
NPTS = 262144
NPAN = 2048
BLOCKS = 4
ROWS = 16384


def draw_points(key, count, low, high):
    first = jax.random.fold_in(key, 0)
    third = jax.random.fold_in(key, 2)
    plane = jax.random.uniform(first, (2, count), dtype=jnp.float32, minval=0.0, maxval=6.0)
    depth = jax.random.uniform(third, (1, count), dtype=jnp.float32, minval=low, maxval=high)
    return jnp.concatenate([plane, depth], 0).astype(jnp.float32)


def draw_row_points(key, part):
    return draw_points(jax.random.fold_in(key, 11), ROWS, 0.0, 0.25)


def draw_source_points(key, part):
    return draw_points(jax.random.fold_in(key, 23), NPTS, -2.5, -0.5)


def draw_admissible(key, part):
    tiles = NPAN // PAN_DEV
    one, two, three, four = jax.random.split(key, 4)
    first = jax.random.randint(one, (BLOCKS, tiles), 0, PAN_DEV + 1)
    second = jax.random.randint(two, (BLOCKS, tiles), 0, PAN_DEV + 1)
    count = first * second // PAN_DEV
    full = jax.random.randint(three, (BLOCKS, 1), 0, tiles)
    count = jnp.where(jnp.arange(tiles)[None, :] == full, PAN_DEV, count)
    scores = jax.random.randint(four, (BLOCKS, tiles, PAN_DEV), 0, 1 << 20) * PAN_DEV + jnp.arange(PAN_DEV)[None, None, :]
    place = jnp.argsort(jnp.argsort(scores, axis=-1, stable=True), axis=-1, stable=True)
    mask = (place < count[:, :, None]).astype(jnp.int32)
    return mask.reshape(BLOCKS, NPAN)


def shard_levels(key, dims, cuts, low, top_value):
    loudness = 1.0
    for axis_at, parts in cuts:
        steps = jax.random.uniform(jax.random.fold_in(jax.random.fold_in(key, 6), axis_at), (parts,), jnp.float32, low / len(cuts), top_value / len(cuts))
        loudness = loudness * jnp.repeat(jnp.exp(steps), dims[axis_at] // parts).reshape((-1,) + (1,) * (len(dims) - 1 - axis_at))
    return loudness


def noise(key, dims, scale, most, pieces=(), held_as=jnp.bfloat16):
    array = jax.random.normal(key, dims, jnp.float32) * scale
    if len(pieces) > 0:
        array = shard_levels(key, dims, pieces, -0.22, 0.18) * array
    return jnp.clip(array, min=-most, max=most).astype(held_as)


def setup_inputs(seed: int = 0) -> dict:
    key_list = jax.random.split(jax.random.key(seed), 5)
    return {
        "row_points": draw_row_points(jax.random.fold_in(key_list[4], 71), 0),
        "source_points": draw_source_points(jax.random.fold_in(key_list[4], 71), 0),
        "sketch": noise(key_list[2], (NPTS, K), 1.0, 6.0, ((0, 64),)),
        "admissible": draw_admissible(jax.random.fold_in(key_list[4], 71), 0),
    }


DAMPING = 0.25
WAVENUM = 24.0

def kernel_block(targets, sources):
    dx = targets[0][:, None] - sources[0][None, :]
    dy = targets[1][:, None] - sources[1][None, :]
    dz = targets[2][:, None] - sources[2][None, :]
    dist = jnp.sqrt(dx * dx + dy * dy + dz * dz)
    value = jnp.exp(-DAMPING * dist) * jnp.cos(WAVENUM * dist) / (4.0 * math.pi * dist)
    return value.astype(jnp.bfloat16)

def factor(gram):
    shift = 0.0001 * jnp.trace(gram) / gram.shape[0]
    return jnp.linalg.cholesky(gram + shift * jnp.eye(gram.shape[0], dtype=jnp.float32))

def reference(row_points, source_points, sketch, admissible):
    pan_src = source_points.reshape(3, NPAN, PW).transpose(1, 0, 2)
    pan_sk = sketch.reshape(NPAN, PW, K)
    blk_pts = row_points.reshape(3, BLOCKS, CS).transpose(1, 0, 2)

    def one_block(item):
        targets, flags = item

        def add_panel(total, entry):
            src, omega, flag = entry
            term = lax.cond(flag > 0, lambda: jnp.dot(kernel_block(targets, src).astype(jnp.float32), omega.astype(jnp.float32), preferred_element_type=jnp.float32), lambda: jnp.zeros((CS, K), jnp.float32))
            return (total + term, None)
        sampled, _ = lax.scan(add_panel, jnp.zeros((CS, K), jnp.float32), (pan_src, pan_sk, flags))
        sampled_low = sampled.astype(jnp.bfloat16)
        gram = jnp.dot(sampled_low.T.astype(jnp.float32), sampled_low.astype(jnp.float32), preferred_element_type=jnp.float32)
        lower = factor(gram)
        basis = jax.scipy.linalg.solve_triangular(lower, sampled_low.astype(jnp.float32).T, lower=True).T
        basis_low = basis.astype(jnp.bfloat16)

        def project(carry, entry):
            src, flag = entry
            out = lax.cond(flag > 0, lambda: jnp.dot(basis_low.T.astype(jnp.float32), kernel_block(targets, src).astype(jnp.float32), preferred_element_type=jnp.float32), lambda: jnp.zeros((K, PW), jnp.float32))
            return (carry, out.astype(jnp.bfloat16))
        _, panels = lax.scan(project, jnp.zeros((), jnp.float32), (pan_src, flags))
        return (basis, panels.transpose(1, 0, 2).reshape(K, NPTS))
    bases, projs = lax.map(one_block, (blk_pts, admissible))
    return (bases.reshape(ROWS, K), projs)
```

```python
import functools
import math

import jax
import jax.numpy as jnp
from jax import lax
from jax.experimental import pallas as pl
from jax.experimental.pallas import tpu as pltpu
from jax.sharding import PartitionSpec as P

DAMPING = 0.25
WAVENUM = 24.0
TURN = WAVENUM / (2.0 * math.pi)
DECAY = -DAMPING * math.log2(math.e) / TURN
SCALE = TURN / (4.0 * math.pi)
HALF_TURN = (0.9999982891022392, -4.934458900946806, 4.048771386943898, -1.2477978368551703)
COEFS = tuple(c * math.sqrt(2.0 * SCALE) for c in HALF_TURN)
F32 = jnp.float32
BF16 = jnp.bfloat16
MESH = pl.DeviceIdType.MESH

CY = 8
KA = 32


def dot(a, b):
    return jnp.dot(a, b, preferred_element_type=F32)


def dot_nt(a, b):
    return lax.dot_general(a, b, (((1,), (1,)), ((), ())), preferred_element_type=F32)


def values(u):
    rs = lax.rsqrt(u)
    t = u * rs
    f = t - jnp.round(t)
    y = f * f
    c = ((COEFS[3] * y + COEFS[2]) * y + COEFS[1]) * y + COEFS[0]
    amp = jnp.exp2(t * DECAY) * rs
    return (amp * (c * c - SCALE)).astype(BF16)


def split3(x):
    hi = x.astype(BF16).astype(F32)
    rem = x - hi
    mid = rem.astype(BF16).astype(F32)
    return hi, mid, rem - mid


def put_aug(tmp, ref, pts, is_source):
    n = pts.shape[1]
    x = (pts[0:1] - 3.0) * TURN
    y = (pts[1:2] - 3.0) * TURN
    z = (pts[2:3] + 1.1) * TURN
    norm = list(split3(x * x + y * y + z * z))
    rows = []
    for v in (x, y, z):
        hi, mid, lo = split3(v)
        if is_source:
            hi, mid, lo = -2.0 * hi, -2.0 * mid, -2.0 * lo
            rows += [hi, mid, hi, mid, lo, hi]
        else:
            rows += [hi, hi, mid, mid, hi, lo]
    ones = [jnp.ones((1, n), F32)] * 3
    rows += ones + norm if is_source else norm + ones
    for r, v in enumerate(rows):
        tmp[r : r + 1, :] = v
    tmp[len(rows) :, :] = jnp.zeros((KA - len(rows), n), F32)
    ref[...] = tmp[...].astype(BF16)


def compact(flags, order, panels):
    def step(g, count):
        order[count] = g
        return count + flags[0, g]

    return lax.fori_loop(0, panels, step, jnp.int32(0))


def sketch_body(group, chunk, flags, tpts, spts, sk, out, cache, order, taug, saug, tmp, tb, skt, buf, sem):
    panels = flags.shape[1]
    width = spts.shape[1] // panels
    rows = taug.shape[1]
    count = compact(flags, order, panels)
    base = pl.multiple_of(lax.axis_index("row") * rows, rows)
    put_aug(tmp, taug, tpts[:, pl.ds(base, rows)], False)
    put_aug(tmp, saug, spts[...], True)
    out[...] = jnp.zeros_like(out)
    steps = (count + group - 1) // group

    def out_copy(i):
        slot = lax.rem(i, 2)
        return pltpu.make_async_copy(buf.at[slot], cache.at[i], sem.at[slot])

    def step(i, _):
        for s in range(group):
            live = i * group + s < count
            g = jnp.where(live, order[i * group + s], 0)
            col = pl.multiple_of(g * width, width)
            tb[s * width : (s + 1) * width, :] = saug[:, pl.ds(col, width)].astype(F32).T.astype(BF16)
            mark = jnp.where(live, 1.0, 0.0)
            skt[:, s * width : (s + 1) * width] = (sk[pl.ds(col, width), :].astype(F32).T * mark).astype(BF16)
        slot = lax.rem(i, 2)

        @pl.when(i >= 2)
        def _():
            out_copy(i - 2).wait()

        for r in range(rows // chunk):
            u = dot(tb[...], taug[:, r * chunk : (r + 1) * chunk])
            v = values(u)
            buf[slot, :, r * chunk : (r + 1) * chunk] = v
            part = dot(skt[...], v)
            span = out.shape[2]
            for q in range(chunk // span):
                out[r * (chunk // span) + q] += part[:, q * span : (q + 1) * span]
        out_copy(i).start()
        return 0

    lax.fori_loop(0, steps, step, 0)

    @pl.when(steps >= 2)
    def _():
        out_copy(steps - 2).wait()

    @pl.when(steps >= 1)
    def _():
        out_copy(steps - 1).wait()


def sum_body(dims, part, out, s1, r1, a1, s2, r2, a2, s3, r3, full, send, recv):
    nz, ny, nc = dims
    me = lax.axis_index("tile")
    c = lax.rem(me, nc)
    y = lax.rem(me // nc, ny)
    z = me // (nc * ny)
    kz = part.shape[1] // nz

    def tile_of(zz, yy, cc):
        return (zz * ny + yy) * nc + cc

    peers = [tile_of(z, y, 1 - c)]
    peers += [tile_of(z, lax.rem(y + o, ny), c) for o in range(1, ny)]
    peers += [tile_of(lax.rem(z + o, nz), y, c) for o in range(1, nz)]
    barrier = pltpu.get_barrier_semaphore()
    for p in peers:
        pl.semaphore_signal(barrier, inc=1, device_id={"tile": p}, device_id_type=MESH)
    pl.semaphore_wait(barrier, len(peers))
    count = [0]

    def push(src, dst, peer):
        n = count[0]
        count[0] += 1
        copy = pltpu.make_async_remote_copy(
            src_ref=src, dst_ref=dst, send_sem=send.at[n], recv_sem=recv.at[n],
            device_id={"tile": peer}, device_id_type=MESH)
        copy.start()
        return copy

    s1[...] = part[pl.ds((1 - c) * ny, ny)].astype(BF16)
    push(s1, r1, peers[0]).wait()
    a1[...] = part[pl.ds(c * ny, ny)] + r1[...].astype(F32)
    s2[...] = a1[...].astype(BF16)
    copies = [push(s2.at[lax.rem(y + o, ny)], r2.at[o - 1], peers[o]) for o in range(1, ny)]
    for copy in copies:
        copy.wait()
    total = a1[y]
    for o in range(1, ny):
        total = total + r2[o - 1].astype(F32)
    for q in range(nz):
        a2[q] = total[q * kz : (q + 1) * kz]
        s3[q] = total[q * kz : (q + 1) * kz].astype(BF16)
    copies = [push(s3.at[lax.rem(z + o, nz)], r3.at[o - 1], peers[ny + o - 1]) for o in range(1, nz)]
    for copy in copies:
        copy.wait()
    total = a2[z]
    for o in range(1, nz):
        total = total + r3[o - 1].astype(F32)
    cy = c * ny + y
    full[cy, z] = total.astype(BF16)
    copies = [push(full.at[cy, z], full.at[cy, z], peers[ny + o - 1]) for o in range(1, nz)]
    for copy in copies:
        copy.wait()
    copies = [push(full.at[cy], full.at[cy], peers[o]) for o in range(1, ny)]
    for copy in copies:
        copy.wait()
    half = full.at[pl.ds(c * ny, ny)]
    push(half, half, peers[0]).wait()
    out[...] = full[...]


def inverse_factor(gram, linv):
    n = gram.shape[0]
    lane = lax.broadcasted_iota(jnp.int32, (1, n), 1)
    left = gram
    ri = lax.broadcasted_iota(jnp.int32, (n, n), 0)
    ci = lax.broadcasted_iota(jnp.int32, (n, n), 1)
    right = (ri == ci).astype(F32)
    for blk in range(n // 8):
        rows = left.shape[0]
        rid = lax.broadcasted_iota(jnp.int32, (rows, 1), 0)
        for jj in range(8):
            j = blk * 8 + jj
            top = left[jj : jj + 1]
            inv = 1.0 / top[:, j : j + 1]
            f = jnp.where(rid > jj, left[:, j : j + 1] * inv, 0.0)
            left = left - f * top
            right = right - f * right[jj : jj + 1]
        sub = lax.broadcasted_iota(jnp.int32, (8, n), 0) + blk * 8
        d = jnp.sum(jnp.where(sub == lane, left[0:8], 0.0), axis=1, keepdims=True)
        linv[blk * 8 : blk * 8 + 8, :] = right[0:8] * lax.rsqrt(d)
        left = left[8:]
        right = right[8:]


def project_body(group, flags, s, cache, basis, proj, order, linv, bf, bl, buf, sem):
    panels = flags.shape[1]
    width = proj.shape[1] // panels
    n = proj.shape[0]
    count = compact(flags, order, panels)
    steps = (count + group - 1) // group

    def in_copy(i):
        slot = lax.rem(i, 2)
        return pltpu.make_async_copy(cache.at[i], buf.at[slot], sem.at[slot])

    @pl.when(steps >= 1)
    def _():
        in_copy(0).start()

    proj[...] = jnp.zeros_like(proj)
    span = s.shape[2]
    gram = dot_nt(s[0], s[0])
    for q in range(1, CY):
        gram = gram + dot_nt(s[q], s[q])
    ri = lax.broadcasted_iota(jnp.int32, (n, n), 0)
    ci = lax.broadcasted_iota(jnp.int32, (n, n), 1)
    eye = (ri == ci).astype(F32)
    shift = 0.0001 * jnp.sum(gram * eye) / n
    inverse_factor(gram + shift * eye, linv)
    pieces = [p.astype(BF16) for p in split3(linv[...])]
    for q in range(CY):
        b = dot(pieces[0], s[q]) + dot(pieces[1], s[q]) + dot(pieces[2], s[q])
        bf[q] = b
        bl[:, q * span : (q + 1) * span] = b.astype(BF16)
    me = lax.axis_index("tile")
    own = basis.shape[0]
    per = span // own
    at = pl.multiple_of(lax.rem(me, per) // 2 * 128, 128)
    block = bf[me // per, :, pl.ds(at, 128)].T
    basis[...] = jnp.where(lax.rem(me, 2) == 0, block[:own], block[own:])

    def step(i, _):
        slot = lax.rem(i, 2)

        @pl.when(i + 1 < steps)
        def _():
            in_copy(i + 1).start()

        in_copy(i).wait()
        o = dot_nt(bl[...], buf[slot]).astype(BF16)
        for k in range(group):

            @pl.when(i * group + k < count)
            def _():
                at = pl.multiple_of(order[i * group + k] * width, width)
                proj[:, pl.ds(at, width)] = o[:, k * width : (k + 1) * width]

        return 0

    lax.fori_loop(0, steps, step, 0)


def local(row_points, source_points, sketch, admissible):
    panels = admissible.shape[1]
    cols = sketch.shape[0]
    width = cols // panels
    n = sketch.shape[1]
    rows = row_points.shape[1] // lax.axis_size("row")
    tiles = lax.axis_size("tile")
    nc, ny = 2, 4
    nz = tiles // (nc * ny)
    span = rows // CY
    group = 2
    vmem = pl.BlockSpec(memory_space=pltpu.VMEM)
    smem = pl.BlockSpec(memory_space=pltpu.SMEM)
    hbm = pl.BlockSpec(memory_space=pl.ANY)
    dma = pltpu.SemaphoreType.DMA
    part, cache = pl.pallas_call(
        functools.partial(sketch_body, group, 2048),
        in_specs=[smem, vmem, vmem, vmem],
        out_specs=[vmem, hbm],
        out_shape=[jax.ShapeDtypeStruct((CY, n, span), F32),
                   jax.ShapeDtypeStruct((panels // group, group * width, rows), BF16)],
        scratch_shapes=[
            pltpu.SMEM((panels + 1,), jnp.int32),
            pltpu.VMEM((KA, rows), BF16), pltpu.VMEM((KA, cols), BF16), pltpu.VMEM((KA, rows), F32),
            pltpu.VMEM((group * width, KA), BF16), pltpu.VMEM((n, group * width), BF16),
            pltpu.VMEM((2, group * width, rows), BF16), dma((2,))],
        compiler_params=pltpu.CompilerParams(vmem_limit_bytes=48 << 20),
        name="sketch",
    )(admissible, row_points, source_points, sketch)
    kz = n // nz
    total = pl.pallas_call(
        functools.partial(sum_body, (nz, ny, nc)),
        in_specs=[vmem],
        out_specs=vmem,
        out_shape=jax.ShapeDtypeStruct((CY, nz, kz, span), BF16),
        scratch_shapes=[
            pltpu.VMEM((ny, n, span), BF16), pltpu.VMEM((ny, n, span), BF16), pltpu.VMEM((ny, n, span), F32),
            pltpu.VMEM((ny, n, span), BF16), pltpu.VMEM((ny - 1, n, span), BF16), pltpu.VMEM((nz, kz, span), F32),
            pltpu.VMEM((nz, kz, span), BF16), pltpu.VMEM((nz - 1, kz, span), BF16),
            pltpu.VMEM((CY, nz, kz, span), BF16), dma((22,)), dma((22,))],
        compiler_params=pltpu.CompilerParams(
            collective_id=0, has_side_effects=True, vmem_limit_bytes=48 << 20),
        name="sum_rows",
    )(part)
    basis, proj = pl.pallas_call(
        functools.partial(project_body, group),
        in_specs=[smem, vmem, hbm],
        out_specs=[vmem, vmem],
        out_shape=[jax.ShapeDtypeStruct((rows // tiles, n), F32), jax.ShapeDtypeStruct((n, cols), BF16)],
        scratch_shapes=[
            pltpu.SMEM((panels + 1,), jnp.int32),
            pltpu.VMEM((n, n), F32), pltpu.VMEM((CY, n, span), F32), pltpu.VMEM((n, rows), BF16),
            pltpu.VMEM((2, group * width, rows), BF16), dma((2,))],
        compiler_params=pltpu.CompilerParams(vmem_limit_bytes=48 << 20),
        name="project",
    )(admissible, total.reshape(CY, n, span), cache)
    return (basis, proj[None])


def solution(mesh):
    in_specs = (P(), P(None, "tile"), P("tile", None), P("row", "tile"))
    out_specs = (P(("row", "tile"), None), P("row", None, "tile"))
    return jax.shard_map(local, mesh=mesh, in_specs=in_specs, out_specs=out_specs, check_vma=False)
```

```python
import functools
import math

import jax
import jax.numpy as jnp
from jax import lax
from jax.experimental import pallas as pl
from jax.experimental.pallas import tpu as pltpu
from jax.sharding import PartitionSpec as P

DAMPING = 0.25
WAVENUM = 24.0
TURN = WAVENUM / (2.0 * math.pi)
DECAY = -DAMPING * math.log2(math.e) / TURN
SCALE = TURN / (4.0 * math.pi)
HALF_TURN = (0.9999982891022392, -4.934458900946806, 4.048771386943898, -1.2477978368551703)
COEFS = tuple(c * math.sqrt(2.0 * SCALE) for c in HALF_TURN)
F32 = jnp.float32
BF16 = jnp.bfloat16
MESH = pl.DeviceIdType.MESH

KA = 32


def dot(a, b):
    return jnp.dot(a, b, preferred_element_type=F32)


def dot_nt(a, b):
    return lax.dot_general(a, b, (((1,), (1,)), ((), ())), preferred_element_type=F32)


def values(u):
    rs = lax.rsqrt(u)
    t = u * rs
    f = t - jnp.round(t)
    y = f * f
    c = ((COEFS[3] * y + COEFS[2]) * y + COEFS[1]) * y + COEFS[0]
    amp = jnp.exp2(t * DECAY) * rs
    return (amp * (c * c - SCALE)).astype(BF16)


def split3(x):
    hi = x.astype(BF16).astype(F32)
    rem = x - hi
    mid = rem.astype(BF16).astype(F32)
    return hi, mid, rem - mid


def put_aug(tmp, ref, pts, is_source):
    n = pts.shape[1]
    x = (pts[0:1] - 3.0) * TURN
    y = (pts[1:2] - 3.0) * TURN
    z = (pts[2:3] + 1.1) * TURN
    norm = list(split3(x * x + y * y + z * z))
    rows = []
    for v in (x, y, z):
        hi, mid, lo = split3(v)
        if is_source:
            hi, mid, lo = -2.0 * hi, -2.0 * mid, -2.0 * lo
            rows += [hi, mid, hi, mid, lo, hi]
        else:
            rows += [hi, hi, mid, mid, hi, lo]
    ones = [jnp.ones((1, n), F32)] * 3
    rows += ones + norm if is_source else norm + ones
    for r, v in enumerate(rows):
        tmp[r : r + 1, :] = v
    tmp[len(rows) :, :] = jnp.zeros((KA - len(rows), n), F32)
    ref[...] = tmp[...].astype(BF16)


def compact(flags, row, order, panels):
    def step(g, count):
        order[row, count] = g
        return count + flags[row, 0, g]

    return lax.fori_loop(0, panels, step, jnp.int32(0))


def prepare_body(own_flags, tpts_hbm, spts_hbm, flags, ta, tr, sa, tpts, trest, spts, tmp, stage, got, send, recv, insem):
    nx = flags.shape[0]
    x = lax.axis_index("row")
    quarter = ta.shape[1] // nx
    rows = nx * quarter

    def piece(b, q, dst, k):
        at = pl.multiple_of(b * rows + q * quarter, quarter)
        return pltpu.make_async_copy(tpts_hbm.at[:, pl.ds(at, quarter)], dst, insem.at[k])

    copies = [piece(b, x, tpts.at[:, b * quarter : (b + 1) * quarter], b) for b in range(nx)]
    copies += [piece(x, lax.rem(x + k, nx), trest.at[:, (k - 1) * quarter : k * quarter], nx + k - 1)
               for k in range(1, nx)]
    copies.append(pltpu.make_async_copy(spts_hbm, spts, insem.at[2 * nx - 1]))
    for copy in copies:
        copy.start()
    stage[...] = jnp.zeros_like(stage)
    stage[0:1, 0 : own_flags.shape[1]] = own_flags[...]
    got[x] = stage[...]
    barrier = pltpu.get_barrier_semaphore()
    peers = [{"row": lax.rem(x + o, nx)} for o in range(1, nx)]
    for p in peers:
        pl.semaphore_signal(barrier, inc=1, device_id=p, device_id_type=MESH)
    pl.semaphore_wait(barrier, len(peers))
    flight = []
    for o, p in enumerate(peers):
        copy = pltpu.make_async_remote_copy(
            src_ref=stage, dst_ref=got.at[x], send_sem=send.at[o], recv_sem=recv.at[o],
            device_id=p, device_id_type=MESH)
        copy.start()
        flight.append(copy)
    for copy in copies:
        copy.wait()
    put_aug(tmp, ta, tpts[...], False)
    put_aug(tmp, sa, spts[...], True)
    put_aug(tmp.at[:, : tr.shape[1]], tr, trest[...], False)
    for copy in flight:
        copy.wait()
    flags[...] = got[...]


def sketch_body(flags_hbm, taug, saug, sk_hbm, out, cache, flags, order, unit, sk, tb, skt, buf, insem, sem):
    blocks, n, quarter = out.shape
    panels = order.shape[1] - 1
    width = saug.shape[1] // panels
    x = lax.axis_index("row")

    copies = [pltpu.make_async_copy(flags_hbm, flags, insem.at[0]), pltpu.make_async_copy(sk_hbm, sk, insem.at[1])]
    for copy in copies:
        copy.start()
    out[...] = jnp.zeros_like(out)
    copies[0].wait()
    total = jnp.int32(0)
    own = jnp.int32(0)
    for k in range(blocks):
        b = lax.rem(x + k, blocks)
        count = compact(flags, b, order, panels)
        pairs = (count + 1) // 2

        def put(i, at, b=b, count=count):
            unit[0, at] = b
            unit[1, at] = order[b, 2 * i]
            unit[2, at] = jnp.where(2 * i + 1 < count, order[b, 2 * i + 1], panels)
            return at + 1

        total = lax.fori_loop(0, pairs, put, total)
        if k == 0:
            own = total
    unit[0, total] = x
    unit[1, total] = panels
    unit[2, total] = panels
    copies[1].wait()

    def run(at, slot):
        b = unit[0, at]
        for s in range(2):
            g = unit[1 + s, at]
            mark = jnp.where(g < panels, 1.0, 0.0)
            col = pl.multiple_of(jnp.minimum(g, panels - 1) * width, width)
            part = slice(s * width, (s + 1) * width)
            tb[slot, part, :] = saug[:, pl.ds(col, width)].astype(F32).T.astype(BF16)
            skt[slot, :, part] = (sk[pl.ds(col, width), :].astype(F32).T * mark).astype(BF16)
        v = values(dot(tb[slot], taug[:, pl.ds(pl.multiple_of(b * quarter, quarter), quarter)]))
        out[b] += dot(skt[slot], v)
        return v

    def keep(i):
        return pltpu.make_async_copy(buf.at[i], cache.at[i], sem.at[i])

    def own_step(i, _):
        buf[i] = run(i, 0)
        keep(i).start()
        return 0

    def other_step(i, _):
        at = own + 2 * i
        run(at, 0)
        run(at + 1, 1)
        return 0

    lax.fori_loop(0, own, own_step, 0)
    lax.fori_loop(0, (total - own + 1) // 2, other_step, 0)

    def done(i, _):
        keep(i).wait()
        return 0

    lax.fori_loop(0, own, done, 0)


def sum_body(dims, shares, part, taug, saug, out, cache, tb, buf,
             s1, r1, a1, s2, r2, s3, a3, r3, low, full, send, recv, sem):
    nx, nz, ny, nc = dims
    me = lax.axis_index("tile")
    x = lax.axis_index("row")
    c = lax.rem(me, nc)
    y = lax.rem(me // nc, ny)
    z = me // (nc * ny)
    n, quarter = part.shape[1], part.shape[2]
    half = quarter // nc
    lanes = half // ny
    kz = n // nz

    def tile_of(zz, yy, cc):
        return {"tile": (zz * ny + yy) * nc + cc}

    core_peer = tile_of(z, y, 1 - c)
    y_peers = [tile_of(z, lax.rem(y + o, ny), c) for o in range(1, ny)]
    z_peers = [tile_of(lax.rem(z + o, nz), y, c) for o in range(1, nz)]
    x_peers = [{"row": lax.rem(x + o, nx)} for o in range(1, nx)]
    barrier = pltpu.get_barrier_semaphore()
    peers = [core_peer] + y_peers + z_peers + x_peers
    for p in peers:
        pl.semaphore_signal(barrier, inc=1, device_id=p, device_id_type=MESH)
    count = [0]

    def push(src, dst, peer):
        k = count[0]
        count[0] += 1
        copy = pltpu.make_async_remote_copy(
            src_ref=src, dst_ref=dst, send_sem=send.at[k], recv_sem=recv.at[k],
            device_id=peer, device_id_type=MESH)
        copy.start()
        return copy

    def keep(i):
        slot = lax.rem(i, 2)
        return pltpu.make_async_copy(buf.at[slot], cache.at[pl.ds(2 * i, 2)], sem.at[slot])

    panels, width = cache.shape[0], cache.shape[1]

    def step(i, _):
        slot = lax.rem(i, 2)

        @pl.when(i >= 2)
        def _():
            keep(i - 2).wait()

        col = pl.multiple_of(i * 2 * width, 2 * width)
        tb[...] = saug[:, pl.ds(col, 2 * width)].astype(F32).T.astype(BF16)
        for r in range(nx - 1):
            v = values(dot(tb[...], taug[:, r * quarter : (r + 1) * quarter]))
            for s in range(2):
                buf[slot, s, :, r * quarter : (r + 1) * quarter] = v[s * width : (s + 1) * width]
        keep(i).start()
        return 0

    edges = [sum(shares[:k]) for k in range(len(shares) + 1)]

    def work(k):
        if edges[k + 1] > edges[k]:
            lax.fori_loop(edges[k], edges[k + 1], step, 0)

    def finish(made):
        for copy in made:
            copy.wait()

    s1[...] = part[:, :, pl.ds(pl.multiple_of((1 - c) * half, half), half)].astype(BF16)
    pl.semaphore_wait(barrier, len(peers))
    flight = [push(s1, r1, core_peer)]
    work(0)
    finish(flight)
    for q in range(ny):
        at = pl.multiple_of(c * half + q * lanes, lanes)
        a = part[:, :, pl.ds(at, lanes)] + r1[:, :, q * lanes : (q + 1) * lanes].astype(F32)
        a1[q] = a
        s2[q] = a.astype(BF16)
    flight = [push(s2.at[lax.rem(y + o, ny)], r2.at[o - 1], y_peers[o - 1]) for o in range(1, ny)]
    work(1)
    finish(flight)
    for q in range(nz):
        cut = slice(q * kz, (q + 1) * kz)
        a = a1[y, :, cut, :]
        for o in range(1, ny):
            a = a + r2[o - 1, :, cut, :].astype(F32)
        a3[q] = a
        s3[q] = a.astype(BF16)
    flight = [push(s3.at[lax.rem(z + o, nz)], r3.at[o - 1], z_peers[o - 1]) for o in range(1, nz)]
    work(2)
    finish(flight)
    a = a3[z]
    for o in range(1, nz):
        a = a + r3[o - 1].astype(F32)
    low[...] = a.astype(BF16)
    full[c, y, z, x] = low[x]
    flight = [push(low.at[lax.rem(x + o, nx)], full.at[c, y, z, x], x_peers[o - 1]) for o in range(1, nx)]
    work(3)
    finish(flight)
    flight = [push(full.at[c, y, z], full.at[c, y, z], p) for p in z_peers]
    work(4)
    finish(flight)
    flight = [push(full.at[c, y], full.at[c, y], p) for p in y_peers]
    work(5)
    finish(flight)
    flight = [push(full.at[c], full.at[c], core_peer)]
    work(6)
    finish(flight)
    out[...] = full[...]
    keep(panels // 2 - 2).wait()
    keep(panels // 2 - 1).wait()


def inverse_factor(gram, linv):
    n = gram.shape[0]
    lane = lax.broadcasted_iota(jnp.int32, (1, n), 1)
    left = gram
    ri = lax.broadcasted_iota(jnp.int32, (n, n), 0)
    ci = lax.broadcasted_iota(jnp.int32, (n, n), 1)
    right = (ri == ci).astype(F32)
    for blk in range(n // 8):
        rows = left.shape[0]
        rid = lax.broadcasted_iota(jnp.int32, (rows, 1), 0)
        for jj in range(8):
            j = blk * 8 + jj
            top = left[jj : jj + 1]
            inv = 1.0 / top[:, j : j + 1]
            f = jnp.where(rid > jj, left[:, j : j + 1] * inv, 0.0)
            left = left - f * top
            right = right - f * right[jj : jj + 1]
        sub = lax.broadcasted_iota(jnp.int32, (8, n), 0) + blk * 8
        d = jnp.sum(jnp.where(sub == lane, left[0:8], 0.0), axis=1, keepdims=True)
        linv[blk * 8 : blk * 8 + 8, :] = right[0:8] * lax.rsqrt(d)
        left = left[8:]
        right = right[8:]


def project_body(flags_hbm, low, own_cache, cache, basis, proj, flags, order, st, linv, bf, bl, own_buf, buf, fsem, sem):
    panels = order.shape[1] - 1
    n, width = proj.shape[0], proj.shape[1] // panels
    nc, ny, nz, nx, kz, lanes = low.shape
    quarter = nc * ny * lanes
    x = lax.axis_index("row")
    copy = pltpu.make_async_copy(flags_hbm, flags, fsem)
    copy.start()
    proj[...] = jnp.zeros_like(proj)
    copy.wait()
    count = compact(flags, x, order, panels)
    steps = (count + 1) // 2

    def in_copies(i):
        slot = lax.rem(i, 2)
        made = [pltpu.make_async_copy(own_cache.at[i], own_buf.at[slot], sem.at[slot, 0])]
        for k in range(2):
            g = jnp.where(2 * i + k < count, order[x, jnp.minimum(2 * i + k, count - 1)], 0)
            made.append(pltpu.make_async_copy(
                cache.at[g], buf.at[slot, k * width : (k + 1) * width], sem.at[slot, 1 + k]))
        return made

    @pl.when(steps >= 1)
    def _():
        for copy in in_copies(0):
            copy.start()

    for k in range(nx):
        q = lax.rem(x + k, nx)
        for c in range(nc):
            for y in range(ny):
                at = k * quarter + (c * ny + y) * lanes
                st[:, at : at + lanes] = low[c, y, :, q].reshape(n, lanes)
    gram = dot_nt(st[...], st[...])
    ri = lax.broadcasted_iota(jnp.int32, (n, n), 0)
    ci = lax.broadcasted_iota(jnp.int32, (n, n), 1)
    eye = (ri == ci).astype(F32)
    shift = 0.0001 * jnp.sum(gram * eye) / n
    inverse_factor(gram + shift * eye, linv)
    pieces = [p.astype(BF16) for p in split3(linv[...])]
    for k in range(nx):
        cut = slice(k * quarter, (k + 1) * quarter)
        s = st[:, cut]
        b = dot(pieces[0], s) + dot(pieces[1], s) + dot(pieces[2], s)
        bf[k] = b
        bl[:, cut] = b.astype(BF16)
    me = lax.axis_index("tile")
    own = basis.shape[0]
    per = quarter // own
    k = lax.rem(me // per - x + nx, nx)
    at = pl.multiple_of(lax.rem(me, per) // 2 * 128, 128)
    block = bf[k, :, pl.ds(at, 128)].T
    basis[...] = jnp.where(lax.rem(me, 2) == 0, block[:own], block[own:])

    def step(i, _):
        slot = lax.rem(i, 2)

        @pl.when(i + 1 < steps)
        def _():
            for copy in in_copies(i + 1):
                copy.start()

        for copy in in_copies(i):
            copy.wait()
        o = dot_nt(bl[:, :quarter], own_buf[slot]) + dot_nt(bl[:, quarter:], buf[slot])
        o = o.astype(BF16)
        for k in range(2):

            @pl.when(2 * i + k < count)
            def _():
                at = pl.multiple_of(order[x, 2 * i + k] * width, width)
                proj[:, pl.ds(at, width)] = o[:, k * width : (k + 1) * width]

        return 0

    lax.fori_loop(0, steps, step, 0)


SHARES = (2, 3, 2, 2, 2, 3, 2)


def local(row_points, source_points, sketch, admissible):
    blocks = lax.axis_size("row")
    panels = admissible.shape[1]
    cols, n = sketch.shape
    width = cols // panels
    rows = row_points.shape[1] // blocks
    quarter = rows // blocks
    tiles = lax.axis_size("tile")
    nc, ny, nx = 2, 4, blocks
    nz = tiles // (nc * ny)
    lanes = quarter // (nc * ny)
    kz = n // nz
    vmem = pl.BlockSpec(memory_space=pltpu.VMEM)
    hbm = pl.BlockSpec(memory_space=pltpu.HBM)
    dma = pltpu.SemaphoreType.DMA
    VM = pltpu.VMEM
    rest = rows - quarter
    flags, ta, tr, sa = pl.pallas_call(
        prepare_body,
        in_specs=[vmem, hbm, hbm],
        out_specs=[vmem] * 4,
        out_shape=[jax.ShapeDtypeStruct((blocks, 8, 128), jnp.int32), jax.ShapeDtypeStruct((KA, rows), BF16),
                   jax.ShapeDtypeStruct((KA, rest), BF16), jax.ShapeDtypeStruct((KA, cols), BF16)],
        scratch_shapes=[
            VM((3, rows), F32), VM((3, rest), F32), VM((3, cols), F32), VM((KA, max(rows, cols)), F32),
            VM((8, 128), jnp.int32), VM((blocks, 8, 128), jnp.int32), dma((nx - 1,)), dma((nx - 1,)), dma((2 * nx,))],
        compiler_params=pltpu.CompilerParams(
            collective_id=1, has_side_effects=True, vmem_limit_bytes=16384 << 10),
        name="prepare",
    )(admissible, row_points, source_points)
    part, own_cache = pl.pallas_call(
        sketch_body,
        in_specs=[hbm, vmem, vmem, hbm],
        out_specs=[vmem, hbm],
        out_shape=[jax.ShapeDtypeStruct((blocks, n, quarter), F32),
                   jax.ShapeDtypeStruct((panels // 2, 2 * width, quarter), BF16)],
        scratch_shapes=[
            pltpu.SMEM((blocks, 8, 128), jnp.int32),
            pltpu.SMEM((blocks, panels + 1), jnp.int32), pltpu.SMEM((3, blocks * panels // 2 + 1), jnp.int32),
            VM((cols, n), BF16),
            VM((2, 2 * width, KA), BF16), VM((2, n, 2 * width), BF16),
            VM((panels // 2, 2 * width, quarter), BF16), dma((2,)), dma((panels // 2,))],
        compiler_params=pltpu.CompilerParams(vmem_limit_bytes=49152 << 10),
        name="sketch",
    )(flags, ta, sa, sketch)
    low, cache = pl.pallas_call(
        functools.partial(sum_body, (nx, nz, ny, nc), SHARES),
        in_specs=[vmem, vmem, vmem],
        out_specs=[vmem, hbm],
        out_shape=[jax.ShapeDtypeStruct((nc, ny, nz, nx, kz, lanes), BF16),
                   jax.ShapeDtypeStruct((panels, width, rest), BF16)],
        scratch_shapes=[
            VM((2 * width, KA), BF16), VM((2, 2, width, rest), BF16),
            VM((blocks, n, quarter // nc), BF16), VM((blocks, n, quarter // nc), BF16),
            VM((ny, blocks, n, lanes), F32), VM((ny, blocks, n, lanes), BF16), VM((ny - 1, blocks, n, lanes), BF16),
            VM((nz, blocks, kz, lanes), BF16), VM((nz, blocks, kz, lanes), F32), VM((nz - 1, blocks, kz, lanes), BF16),
            VM((blocks, kz, lanes), BF16), VM((nc, ny, nz, nx, kz, lanes), BF16),
            dma((25,)), dma((25,)), dma((2,))],
        compiler_params=pltpu.CompilerParams(
            collective_id=0, has_side_effects=True, vmem_limit_bytes=48 << 20),
        name="sum_rows",
    )(part, tr, sa)
    basis, proj = pl.pallas_call(
        project_body,
        in_specs=[hbm, vmem, hbm, hbm],
        out_specs=[vmem, vmem],
        out_shape=[jax.ShapeDtypeStruct((rows // tiles, n), F32), jax.ShapeDtypeStruct((n, cols), BF16)],
        scratch_shapes=[
            pltpu.SMEM((blocks, 8, 128), jnp.int32), pltpu.SMEM((blocks, panels + 1), jnp.int32),
            VM((n, rows), BF16), VM((n, n), F32), VM((nx, n, quarter), F32), VM((n, rows), BF16),
            VM((2, 2 * width, quarter), BF16), VM((2, 2 * width, rest), BF16), dma, dma((2, 3))],
        compiler_params=pltpu.CompilerParams(vmem_limit_bytes=48 << 20),
        name="project",
    )(flags, low, own_cache, cache)
    return (basis, proj[None])


def solution(mesh):
    in_specs = (P(), P(None, "tile"), P("tile", None), P("row", "tile"))
    out_specs = (P(("row", "tile"), None), P("row", None, "tile"))
    return jax.shard_map(local, mesh=mesh, in_specs=in_specs, out_specs=out_specs, check_vma=False)
```

```python
import functools
import math

import jax
import jax.numpy as jnp
from jax import lax
from jax.experimental import pallas as pl
from jax.experimental.pallas import tpu as pltpu
from jax.sharding import PartitionSpec as P

DAMPING = 0.25
WAVENUM = 24.0
TURN = WAVENUM / (2.0 * math.pi)
DECAY = -DAMPING * math.log2(math.e) / TURN
SCALE = TURN / (4.0 * math.pi)
HALF_TURN = (0.9999982891022392, -4.934458900946806, 4.048771386943898, -1.2477978368551703)
COEFS = tuple(c * math.sqrt(2.0 * SCALE) for c in HALF_TURN)
F32 = jnp.float32
BF16 = jnp.bfloat16
MESH = pl.DeviceIdType.MESH

KA = 32
CHUNK = 256
SIZES = (8, 2)


def dot(a, b):
    return jnp.dot(a, b, preferred_element_type=F32)


def dot_nt(a, b):
    return lax.dot_general(a, b, (((1,), (1,)), ((), ())), preferred_element_type=F32)


def values(u):
    rs = lax.rsqrt(u)
    t = u * rs
    f = t - jnp.round(t)
    y = f * f
    c = ((COEFS[3] * y + COEFS[2]) * y + COEFS[1]) * y + COEFS[0]
    amp = jnp.exp2(t * DECAY) * rs
    return (amp * (c * c - SCALE)).astype(BF16)


def split3(x):
    hi = x.astype(BF16).astype(F32)
    rem = x - hi
    mid = rem.astype(BF16).astype(F32)
    return hi, mid, rem - mid


def put_aug(tmp, ref, pts, is_source):
    fill_aug(tmp, pts, is_source)
    ref[...] = tmp[...].astype(BF16)


def fill_aug(tmp, pts, is_source):
    n = pts.shape[1]
    x = (pts[0:1] - 3.0) * TURN
    y = (pts[1:2] - 3.0) * TURN
    z = (pts[2:3] + 1.1) * TURN
    norm = list(split3(x * x + y * y + z * z))
    rows = []
    for v in (x, y, z):
        hi, mid, lo = split3(v)
        if is_source:
            hi, mid, lo = -2.0 * hi, -2.0 * mid, -2.0 * lo
            rows += [hi, mid, hi, mid, lo, hi]
        else:
            rows += [hi, hi, mid, mid, hi, lo]
    ones = [jnp.ones((1, n), F32)] * 3
    rows += ones + norm if is_source else norm + ones
    for r, v in enumerate(rows):
        tmp[r : r + 1, :] = v
    tmp[len(rows) :, :] = jnp.zeros((KA - len(rows), n), F32)


def compact(flags, row, order, panels):
    def step(g, count):
        order[row, count] = g
        return count + flags[row, 0, g]

    return lax.fori_loop(0, panels, step, jnp.int32(0))


def prepare_body(own_flags, tpts_hbm, spts_hbm, sk_hbm, flags, ta, tr, sa, skt, tpts, trest, spts, sk, tmp, stage, got,
                 send, recv, insem):
    nx = flags.shape[0]
    x = lax.axis_index("row")
    quarter = ta.shape[1] // nx
    rows = nx * quarter

    def piece(b, q, dst, k):
        at = pl.multiple_of(b * rows + q * quarter, quarter)
        return pltpu.make_async_copy(tpts_hbm.at[:, pl.ds(at, quarter)], dst, insem.at[k])

    copies = [piece(b, x, tpts.at[:, b * quarter : (b + 1) * quarter], b) for b in range(nx)]
    copies += [piece(x, lax.rem(x + k, nx), trest.at[:, (k - 1) * quarter : k * quarter], nx + k - 1)
               for k in range(1, nx)]
    copies.append(pltpu.make_async_copy(spts_hbm, spts, insem.at[2 * nx - 1]))
    copies.append(pltpu.make_async_copy(sk_hbm, sk, insem.at[2 * nx]))
    for copy in copies:
        copy.start()
    stage[...] = jnp.zeros_like(stage)
    stage[0:1, 0 : own_flags.shape[1]] = own_flags[...]
    got[x] = stage[...]
    barrier = pltpu.get_barrier_semaphore()
    peers = [{"row": lax.rem(x + o, nx)} for o in range(1, nx)]
    for p in peers:
        pl.semaphore_signal(barrier, inc=1, device_id=p, device_id_type=MESH)
    pl.semaphore_wait(barrier, len(peers))
    flight = []
    for o, p in enumerate(peers):
        copy = pltpu.make_async_remote_copy(
            src_ref=stage, dst_ref=got.at[x], send_sem=send.at[o], recv_sem=recv.at[o],
            device_id=p, device_id_type=MESH)
        copy.start()
        flight.append(copy)
    for copy in copies[:-1]:
        copy.wait()
    put_aug(tmp, ta, tpts[...], False)
    put_aug(tmp.at[:, : tr.shape[1]], tr, trest[...], False)
    fill_aug(tmp, spts[...], True)
    copies[-1].wait()

    def turn(i, _):
        at = pl.ds(pl.multiple_of(i * 128, 128), 128)
        sa[at, :] = tmp[:, at].T.astype(BF16)
        skt[:, at] = sk[at, :].astype(F32).T.astype(BF16)
        return 0

    lax.fori_loop(0, sk.shape[0] // 128, turn, 0, unroll=4)
    for copy in flight:
        copy.wait()
    flags[...] = got[...]


def sketch_body(flags_hbm, taug, saug, skta, out, cache, flags, order, unit, tb, skt, skp, u0, u1, v0, v1, buf, insem, sem):
    us, vs = (u0, u1), (v0, v1)
    blocks, n, quarter = out.shape
    panels = order.shape[1] - 1
    width = saug.shape[0] // panels
    x = lax.axis_index("row")

    flag_copy = pltpu.make_async_copy(flags_hbm, flags, insem)
    flag_copy.start()
    out[...] = jnp.zeros_like(out)
    flag_copy.wait()
    total = jnp.int32(0)
    own = jnp.int32(0)
    for k in range(blocks):
        b = lax.rem(x + k, blocks)
        count = compact(flags, b, order, panels)
        pairs = (count + 1) // 2

        def put(i, at, b=b, count=count):
            unit[0, at] = b
            unit[1, at] = order[b, 2 * i]
            unit[2, at] = jnp.where(2 * i + 1 < count, order[b, 2 * i + 1], panels)
            return at + 1

        total = lax.fori_loop(0, pairs, put, total)
        if k == 0:
            own = total
    for k in range(2):
        unit[0, total + k] = x
        unit[1, total + k] = panels
        unit[2, total + k] = panels

    def ready(at, k):
        for h in range(2):
            g = unit[1 + h, at]
            mark = jnp.where(g < panels, 1.0, 0.0).astype(BF16)
            col = pl.multiple_of(jnp.minimum(g, panels - 1) * width, width)
            part = slice(h * width, (h + 1) * width)
            tb[k, part, :] = saug[pl.ds(col, width), :]
            skt[k, :, part] = skta[:, pl.ds(col, width)] * mark

    def lanes_of(b, r):
        return pl.ds(pl.multiple_of(b * quarter + r * CHUNK, CHUNK), CHUNK)

    def stage(at, k):
        prev, nxt = unit[0, jnp.maximum(at - 1, 0)], unit[0, at + 1]
        ready(at + 1, 1 - k)
        for r in range(quarter // CHUNK):
            cut = slice(r * CHUNK, (r + 1) * CHUNK)
            us[1 - k][:, cut] = dot(tb[1 - k], taug[:, lanes_of(nxt, r)])
            vs[k][:, cut] = values(us[k][:, cut])
            out[prev, :, cut] += dot(skp[k], vs[1 - k][:, cut])
        skp[1 - k] = skt[k]

    def keep(i, k):
        g = unit[1 + k, i]
        return (i < own) & (g < panels), pltpu.make_async_copy(
            buf.at[i, k * width : (k + 1) * width], cache.at[jnp.minimum(g, panels - 1)], sem.at[i, k])

    def own_stage(at, k):
        stage(at, k)
        buf[jnp.minimum(at, panels // 2)] = vs[k][...]
        for h in range(2):
            live, copy = keep(jnp.minimum(at, panels // 2 - 1), h)
            pl.when(live & (at < own))(copy.start)

    ready(0, 0)
    us[0][...] = dot(tb[0], taug[:, pl.ds(pl.multiple_of(unit[0, 0] * quarter, quarter), quarter)])
    skp[0] = jnp.zeros_like(skp[0])
    vs[1][...] = jnp.zeros_like(vs[1])

    def own_step(i, _):
        own_stage(2 * i, 0)
        own_stage(2 * i + 1, 1)
        return 0

    def other_step(size, start, i, _):
        for k in range(size):
            stage(start + size * i + k, k % 2)
        return 0

    turns = (total + 1) // 2
    own_turns = (own + 1) // 2
    lax.fori_loop(0, own_turns, own_step, 0)
    left = 2 * own_turns
    for size in SIZES:
        many = jnp.maximum(2 * turns - left, 0) // size
        lax.fori_loop(0, many, functools.partial(other_step, size, left), 0)
        left = left + many * size
    last = unit[0, jnp.maximum(2 * turns - 1, 0)]
    out[last] += dot(skp[0], vs[1][...])

    def done(i, _):
        for k in range(2):
            live, copy = keep(i, k)
            pl.when(live)(copy.wait)
        return 0

    lax.fori_loop(0, own, done, 0)


def sum_body(dims, shares, part, taug, saug, out, cache, buf,
             s1, r1, a1, s2, r2, s3, a3, r3, low, full, send, recv, sem):
    nx, nz, ny, nc = dims
    me = lax.axis_index("tile")
    x = lax.axis_index("row")
    c = lax.rem(me, nc)
    y = lax.rem(me // nc, ny)
    z = me // (nc * ny)
    n, quarter = part.shape[1], part.shape[2]
    half = quarter // nc
    lanes = half // ny
    kz = n // nz

    def tile_of(zz, yy, cc):
        return {"tile": (zz * ny + yy) * nc + cc}

    core_peer = tile_of(z, y, 1 - c)
    y_peers = [tile_of(z, lax.rem(y + o, ny), c) for o in range(1, ny)]
    z_peers = [tile_of(lax.rem(z + o, nz), y, c) for o in range(1, nz)]
    x_peers = [{"row": lax.rem(x + o, nx)} for o in range(1, nx)]
    barrier = pltpu.get_barrier_semaphore()
    peers = [core_peer] + y_peers + z_peers + x_peers
    for p in peers:
        pl.semaphore_signal(barrier, inc=1, device_id=p, device_id_type=MESH)
    count = [0]

    def push(src, dst, peer):
        k = count[0]
        count[0] += 1
        copy = pltpu.make_async_remote_copy(
            src_ref=src, dst_ref=dst, send_sem=send.at[k], recv_sem=recv.at[k],
            device_id=peer, device_id_type=MESH)
        copy.start()
        return copy

    def keep(i):
        slot = lax.rem(i, 2)
        return pltpu.make_async_copy(buf.at[slot], cache.at[pl.ds(2 * i, 2)], sem.at[slot])

    panels, width = cache.shape[0], cache.shape[1]

    def step(i, _):
        slot = lax.rem(i, 2)

        @pl.when(i >= 2)
        def _():
            keep(i - 2).wait()

        col = pl.multiple_of(i * 2 * width, 2 * width)
        tb = saug.at[pl.ds(col, 2 * width)]
        for r in range(nx - 1):
            v = values(dot(tb[...], taug[:, r * quarter : (r + 1) * quarter]))
            for s in range(2):
                buf[slot, s, :, r * quarter : (r + 1) * quarter] = v[s * width : (s + 1) * width]
        keep(i).start()
        return 0

    edges = [sum(shares[:k]) for k in range(len(shares) + 1)]

    def work(k):
        if edges[k + 1] > edges[k]:
            lax.fori_loop(edges[k], edges[k + 1], step, 0)

    def finish(made):
        for copy in made:
            copy.wait()

    s1[...] = part[:, :, pl.ds(pl.multiple_of((1 - c) * half, half), half)].astype(BF16)
    pl.semaphore_wait(barrier, len(peers))
    flight = [push(s1, r1, core_peer)]
    work(0)
    finish(flight)
    for q in range(ny):
        at = pl.multiple_of(c * half + q * lanes, lanes)
        a = part[:, :, pl.ds(at, lanes)] + r1[:, :, q * lanes : (q + 1) * lanes].astype(F32)
        a1[q] = a
        s2[q] = a.astype(BF16)
    flight = [push(s2.at[lax.rem(y + o, ny)], r2.at[o - 1], y_peers[o - 1]) for o in range(1, ny)]
    work(1)
    finish(flight)
    for q in range(nz):
        cut = slice(q * kz, (q + 1) * kz)
        a = a1[y, :, cut, :]
        for o in range(1, ny):
            a = a + r2[o - 1, :, cut, :].astype(F32)
        a3[q] = a
        s3[q] = a.astype(BF16)
    flight = [push(s3.at[lax.rem(z + o, nz)], r3.at[o - 1], z_peers[o - 1]) for o in range(1, nz)]
    work(2)
    finish(flight)
    a = a3[z]
    for o in range(1, nz):
        a = a + r3[o - 1].astype(F32)
    low[...] = a.astype(BF16)
    full[c, y, z, x] = low[x]
    flight = [push(low.at[lax.rem(x + o, nx)], full.at[c, y, z, x], x_peers[o - 1]) for o in range(1, nx)]
    work(3)
    finish(flight)
    flight = [push(full.at[c, y, z], full.at[c, y, z], p) for p in z_peers]
    work(4)
    finish(flight)
    flight = [push(full.at[c, y], full.at[c, y], p) for p in y_peers]
    work(5)
    finish(flight)
    flight = [push(full.at[c], full.at[c], core_peer)]
    work(6)
    finish(flight)
    out[...] = full[...]
    keep(panels // 2 - 2).wait()
    keep(panels // 2 - 1).wait()


def eliminate(blk, left, right, linv):
    n = left.shape[0]
    at = pl.multiple_of(blk * 8, 8)
    low, inv = left[...], right[...]
    rid = lax.broadcasted_iota(jnp.int32, (n, 1), 0)
    rows, gains = left[pl.ds(at, 8), :], right[pl.ds(at, 8), :]
    r8 = lax.broadcasted_iota(jnp.int32, (8, 1), 0)
    for j in range(8):
        top, gain = rows[j : j + 1], gains[j : j + 1]
        scale = 1.0 / top[:, j : j + 1]
        f8 = jnp.where(r8 > j, rows[:, j : j + 1] * scale, 0.0)
        f = jnp.where(rid >= at + 8, low[:, j : j + 1] * scale, 0.0)
        rows = rows - f8 * top
        gains = gains - f8 * gain
        low = low - f * top
        inv = inv - f * gain
    left[...] = pltpu.roll(low, n - 8, 1)
    right[...] = inv
    lane = lax.broadcasted_iota(jnp.int32, (8, n), 1)
    d = jnp.sum(jnp.where(lane == r8, rows, 0.0), axis=1, keepdims=True)
    linv[pl.ds(at, 8), :] = gains * lax.rsqrt(d)


def dot_full(a, b):
    return jnp.dot(a, b, precision=lax.Precision.HIGHEST, preferred_element_type=F32)


DEPTH = 3


def project_body(flags_hbm, low, own_cache, cache, basis, proj, flags, st, left, right, linv, z, own_buf, buf, fsem, sem):
    panels, width = cache.shape[0], cache.shape[1]
    n = proj.shape[0]
    nc, ny, nz, nx, kz, lanes = low.shape
    quarter = nc * ny * lanes
    steps = panels // 2
    x = lax.axis_index("row")

    def in_copies(i):
        slot = lax.rem(i, DEPTH)
        two = pl.ds(2 * i, 2)
        return [pltpu.make_async_copy(own_cache.at[two], own_buf.at[slot], sem.at[slot, 0]),
                pltpu.make_async_copy(cache.at[two], buf.at[slot], sem.at[slot, 1])]

    flag_copy = pltpu.make_async_copy(flags_hbm, flags, fsem)
    flag_copy.start()
    for i in range(DEPTH - 1):
        for copy in in_copies(i):
            copy.start()
    for k in range(nx):
        q = lax.rem(x + k, nx)
        for c in range(nc):
            for y in range(ny):
                at = k * quarter + (c * ny + y) * lanes
                st[:, at : at + lanes] = low[c, y, :, q].reshape(n, lanes)
    gram = dot_nt(st[...], st[...])
    ri = lax.broadcasted_iota(jnp.int32, (n, n), 0)
    ci = lax.broadcasted_iota(jnp.int32, (n, n), 1)
    eye = (ri == ci).astype(F32)
    shift = 0.0001 * jnp.sum(gram * eye) / n
    left[...] = gram + shift * eye
    right[...] = eye

    def step(i, _):
        slot = lax.rem(i, DEPTH)

        @pl.when(i + DEPTH - 1 < steps)
        def _():
            for copy in in_copies(i + DEPTH - 1):
                copy.start()

        for copy in in_copies(i):
            copy.wait()
        own = own_buf[slot].reshape(2 * width, quarter)
        rest = buf[slot].reshape(2 * width, (nx - 1) * quarter)
        o = dot_nt(st[:, :quarter], own) + dot_nt(st[:, quarter:], rest)
        z[:, pl.ds(pl.multiple_of(i * 2 * width, 2 * width), 2 * width)] = o
        eliminate(i, left, right, linv)
        return 0

    lax.fori_loop(0, steps, step, 0)
    flag_copy.wait()
    factor = linv[...]
    me = lax.axis_index("tile")
    own = basis.shape[0]
    per = quarter // own
    k = lax.rem(me // per - x + nx, nx)
    at = pl.multiple_of(k * quarter + lax.rem(me, per) // 2 * 128, 128)
    block = dot_full(factor, st[:, pl.ds(at, 128)].astype(F32)).T
    basis[...] = jnp.where(lax.rem(me, 2) == 0, block[:own], block[own:])
    for g in range(panels):
        cut = slice(g * width, (g + 1) * width)
        o = dot_full(factor, z[:, cut])
        proj[:, cut] = jnp.where(flags[x, 0, g] > 0, o, 0.0).astype(BF16)


SHARES = (2, 3, 2, 2, 2, 3, 2)


def local(row_points, source_points, sketch, admissible):
    blocks = lax.axis_size("row")
    panels = admissible.shape[1]
    cols, n = sketch.shape
    width = cols // panels
    rows = row_points.shape[1] // blocks
    quarter = rows // blocks
    tiles = lax.axis_size("tile")
    nc, ny, nx = 2, 4, blocks
    nz = tiles // (nc * ny)
    lanes = quarter // (nc * ny)
    kz = n // nz
    vmem = pl.BlockSpec(memory_space=pltpu.VMEM)
    hbm = pl.BlockSpec(memory_space=pltpu.HBM)
    dma = pltpu.SemaphoreType.DMA
    VM = pltpu.VMEM
    rest = rows - quarter
    flags, ta, tr, sa, skt = pl.pallas_call(
        prepare_body,
        in_specs=[vmem, hbm, hbm, hbm],
        out_specs=[vmem] * 5,
        out_shape=[jax.ShapeDtypeStruct((blocks, 8, 128), jnp.int32), jax.ShapeDtypeStruct((KA, rows), BF16),
                   jax.ShapeDtypeStruct((KA, rest), BF16), jax.ShapeDtypeStruct((cols, KA), BF16),
                   jax.ShapeDtypeStruct((n, cols), BF16)],
        scratch_shapes=[
            VM((3, rows), F32), VM((3, rest), F32), VM((3, cols), F32), VM((cols, n), BF16), VM((KA, max(rows, cols)), F32),
            VM((8, 128), jnp.int32), VM((blocks, 8, 128), jnp.int32), dma((nx - 1,)), dma((nx - 1,)), dma((2 * nx + 1,))],
        compiler_params=pltpu.CompilerParams(
            collective_id=1, has_side_effects=True, vmem_limit_bytes=16384 << 10),
        name="prepare",
    )(admissible, row_points, source_points, sketch)
    part, own_cache = pl.pallas_call(
        sketch_body,
        in_specs=[hbm, vmem, vmem, vmem],
        out_specs=[vmem, hbm],
        out_shape=[jax.ShapeDtypeStruct((blocks, n, quarter), F32),
                   jax.ShapeDtypeStruct((panels, width, quarter), BF16)],
        scratch_shapes=[
            pltpu.SMEM((blocks, 8, 128), jnp.int32),
            pltpu.SMEM((blocks, panels + 1), jnp.int32), pltpu.SMEM((3, blocks * panels // 2 + 2), jnp.int32),
            VM((2, 2 * width, KA), BF16), VM((2, n, 2 * width), BF16), VM((2, n, 2 * width), BF16),
            VM((2 * width, quarter), F32), VM((2 * width, quarter), F32),
            VM((2 * width, quarter), BF16), VM((2 * width, quarter), BF16),
            VM((panels // 2 + 1, 2 * width, quarter), BF16), dma, dma((panels // 2, 2))],
        compiler_params=pltpu.CompilerParams(vmem_limit_bytes=49152 << 10),
        name="sketch",
    )(flags, ta, sa, skt)
    low, cache = pl.pallas_call(
        functools.partial(sum_body, (nx, nz, ny, nc), SHARES),
        in_specs=[vmem, vmem, vmem],
        out_specs=[vmem, hbm],
        out_shape=[jax.ShapeDtypeStruct((nc, ny, nz, nx, kz, lanes), BF16),
                   jax.ShapeDtypeStruct((panels, width, rest), BF16)],
        scratch_shapes=[
            VM((2, 2, width, rest), BF16),
            VM((blocks, n, quarter // nc), BF16), VM((blocks, n, quarter // nc), BF16),
            VM((ny, blocks, n, lanes), F32), VM((ny, blocks, n, lanes), BF16), VM((ny - 1, blocks, n, lanes), BF16),
            VM((nz, blocks, kz, lanes), BF16), VM((nz, blocks, kz, lanes), F32), VM((nz - 1, blocks, kz, lanes), BF16),
            VM((blocks, kz, lanes), BF16), VM((nc, ny, nz, nx, kz, lanes), BF16),
            dma((25,)), dma((25,)), dma((2,))],
        compiler_params=pltpu.CompilerParams(
            collective_id=0, has_side_effects=True, vmem_limit_bytes=48 << 20),
        name="sum_rows",
    )(part, tr, sa)
    basis, proj = pl.pallas_call(
        project_body,
        in_specs=[hbm, vmem, hbm, hbm],
        out_specs=[vmem, vmem],
        out_shape=[jax.ShapeDtypeStruct((rows // tiles, n), F32), jax.ShapeDtypeStruct((n, cols), BF16)],
        scratch_shapes=[
            pltpu.SMEM((blocks, 8, 128), jnp.int32),
            VM((n, rows), BF16), VM((n, n), F32), VM((n, n), F32), VM((n, n), F32), VM((n, cols), F32),
            VM((DEPTH, 2, width, quarter), BF16), VM((DEPTH, 2, width, rest), BF16), dma, dma((DEPTH, 2))],
        compiler_params=pltpu.CompilerParams(vmem_limit_bytes=48 << 20),
        name="project",
    )(flags, low, own_cache, cache)
    return (basis, proj[None])


def solution(mesh):
    in_specs = (P(), P(None, "tile"), P("tile", None), P("row", "tile"))
    out_specs = (P(("row", "tile"), None), P("row", None, "tile"))
    return jax.shard_map(local, mesh=mesh, in_specs=in_specs, out_specs=out_specs, check_vma=False)
```

```python
import functools
import math

import jax
import jax.numpy as jnp
from jax import lax
from jax.experimental import pallas as pl
from jax.experimental.pallas import tpu as pltpu
from jax.sharding import PartitionSpec as P

DAMPING = 0.25
WAVENUM = 24.0
TURN = WAVENUM / (2.0 * math.pi)
DECAY = -DAMPING * math.log2(math.e) / TURN
SCALE = TURN / (4.0 * math.pi)
HALF_TURN = (0.9999982891022392, -4.934458900946806, 4.048771386943898, -1.2477978368551703)
COEFS = tuple(c * math.sqrt(2.0 * SCALE) for c in HALF_TURN)
F32 = jnp.float32
BF16 = jnp.bfloat16
MESH = pl.DeviceIdType.MESH

KA = 32
CHUNK = 256
SIZES = (4, 2)
GROUP = 4


def dot(a, b):
    return jnp.dot(a, b, preferred_element_type=F32)


def dot_nt(a, b):
    return lax.dot_general(a, b, (((1,), (1,)), ((), ())), preferred_element_type=F32)


def values(u):
    rs = lax.rsqrt(u)
    t = u * rs
    f = t - jnp.round(t)
    y = f * f
    c = ((COEFS[3] * y + COEFS[2]) * y + COEFS[1]) * y + COEFS[0]
    amp = jnp.exp2(t * DECAY) * rs
    return (amp * (c * c - SCALE)).astype(BF16)


def split3(x):
    hi = x.astype(BF16).astype(F32)
    rem = x - hi
    mid = rem.astype(BF16).astype(F32)
    return hi, mid, rem - mid


def put_aug(tmp, ref, pts, is_source):
    fill_aug(tmp, pts, is_source)
    ref[...] = tmp[...].astype(BF16)


def fill_aug(tmp, pts, is_source):
    n = pts.shape[1]
    x = (pts[0:1] - 3.0) * TURN
    y = (pts[1:2] - 3.0) * TURN
    z = (pts[2:3] + 1.1) * TURN
    norm = list(split3(x * x + y * y + z * z))
    rows = []
    for v in (x, y, z):
        hi, mid, lo = split3(v)
        if is_source:
            hi, mid, lo = -2.0 * hi, -2.0 * mid, -2.0 * lo
            rows += [hi, mid, hi, mid, lo, hi]
        else:
            rows += [hi, hi, mid, mid, hi, lo]
    ones = [jnp.ones((1, n), F32)] * 3
    rows += ones + norm if is_source else norm + ones
    for r, v in enumerate(rows):
        tmp[r : r + 1, :] = v
    tmp[len(rows) :, :] = jnp.zeros((KA - len(rows), n), F32)


def prepare_body(own_flags, tpts_hbm, spts_hbm, sk_hbm, flags, ta, tr, tq, sa, skt,
                 tpts, trest, spts, sk, tmp, stage, got, sa_got, sk_got, send, recv, insem):
    nx, nc = flags.shape[0], flags.shape[1]
    x = lax.axis_index("row")
    me = lax.axis_index("tile")
    c = lax.rem(me, nc)
    half = ta.shape[1] // nx
    quarter = half * nc
    rows = nx * quarter
    panels, width = skt.shape[0] // nc, skt.shape[1]

    def piece(b, at, size, dst, k):
        at = pl.multiple_of(b * rows + at, size)
        return pltpu.make_async_copy(tpts_hbm.at[:, pl.ds(at, size)], dst, insem.at[k])

    copies = [piece(b, x * quarter + c * half, half, tpts.at[:, b * half : (b + 1) * half], b) for b in range(nx)]
    copies += [piece(x, lax.rem(x + k, nx) * quarter, quarter, trest.at[:, k * quarter : (k + 1) * quarter], nx + k)
               for k in range(nx)]
    copies.append(pltpu.make_async_copy(spts_hbm, spts, insem.at[2 * nx]))
    copies.append(pltpu.make_async_copy(sk_hbm, sk, insem.at[2 * nx + 1]))
    for copy in copies:
        copy.start()
    barrier = pltpu.get_barrier_semaphore()
    peers = [(o, k) for o in range(nx) for k in range(nc) if o or k]

    def device(o, k):
        return {"row": lax.rem(x + o, nx), "tile": me - c + lax.rem(c + k, nc)}

    for p in peers:
        pl.semaphore_signal(barrier, inc=1, device_id=device(*p), device_id_type=MESH)
    stage[...] = jnp.zeros_like(stage)
    stage[0:1, 0 : own_flags.shape[1]] = own_flags[...]
    got[x, c] = stage[...]
    flight = []

    def push(src, dst, p):
        n = len(flight)
        copy = pltpu.make_async_remote_copy(
            src_ref=src, dst_ref=dst, send_sem=send.at[n], recv_sem=recv.at[n],
            device_id=device(*p), device_id_type=MESH)
        copy.start()
        flight.append(copy)

    pl.semaphore_wait(barrier, len(peers))
    for p in peers:
        push(stage, got.at[x, c], p)
    for copy in copies[2 * nx :]:
        copy.wait()
    fill_aug(tmp, spts[...], True)
    cols = panels * width

    def turn(i, _):
        at = pl.ds(pl.multiple_of(i * width, width), width)
        sa[pl.ds(pl.multiple_of(c * cols + i * width, width), width), :] = tmp[:, at].T.astype(BF16)
        skt[c * panels + i] = sk[at, :].astype(F32).T.astype(BF16)
        return 0

    lax.fori_loop(0, panels, turn, 0, unroll=4)
    push(sa.at[pl.ds(pl.multiple_of(c * cols, cols), cols)], sa_got, (0, 1))
    push(skt.at[pl.ds(c * panels, panels)], sk_got, (0, 1))
    for copy in copies[: 2 * nx]:
        copy.wait()
    put_aug(tmp.at[:, : ta.shape[1]], ta, tpts[...], False)
    fill_aug(tmp, trest[...], False)
    tq[...] = tmp[:, :quarter].astype(BF16)
    tr[...] = tmp[:, quarter:].astype(BF16)
    for copy in flight:
        copy.wait()
    flags[...] = got[...]
    sa[pl.ds(pl.multiple_of((1 - c) * cols, cols), cols)] = sa_got[...]
    skt[pl.ds((1 - c) * panels, panels)] = sk_got[...]


def sketch_body(flags_hbm, taug, saug, skta, out, flags, order, unit, tb, skt, skp, u0, u1, v0, v1, insem):
    us, vs = (u0, u1), (v0, v1)
    blocks, n, half = out.shape
    nc = flags.shape[1]
    panels, width = skta.shape[0], skta.shape[1]
    per = panels // nc

    flag_copy = pltpu.make_async_copy(flags_hbm, flags, insem)
    flag_copy.start()
    out[...] = jnp.zeros_like(out)
    flag_copy.wait()
    total = jnp.int32(0)
    for b in range(blocks):

        def note(g, count, b=b):
            order[count] = g
            return count + flags[b, g // per, 0, g % per]

        count = lax.fori_loop(0, panels, note, jnp.int32(0))

        def put(i, at, b=b, count=count):
            unit[0, at] = b
            for h in range(GROUP):
                k = GROUP * i + h
                unit[1 + h, at] = jnp.where(k < count, order[jnp.minimum(k, panels)], panels)
            return at + 1

        total = lax.fori_loop(0, (count + GROUP - 1) // GROUP, put, total)
    for k in range(2):
        for h in range(GROUP + 1):
            unit[h, total + k] = panels if h else 0

    def ready(at, k):
        for h in range(GROUP):
            g = unit[1 + h, at]
            mark = jnp.where(g < panels, 1.0, 0.0).astype(BF16)
            g = jnp.minimum(g, panels - 1)
            part = slice(h * width, (h + 1) * width)
            tb[k, part, :] = saug[pl.ds(pl.multiple_of(g * width, width), width), :]
            skt[k, :, part] = skta[g] * mark

    def lanes_of(b, r):
        return pl.ds(pl.multiple_of(b * half + r * CHUNK, CHUNK), CHUNK)

    def stage(at, k):
        prev, nxt = unit[0, jnp.maximum(at - 1, 0)], unit[0, at + 1]
        ready(at + 1, 1 - k)
        for r in range(half // CHUNK):
            cut = slice(r * CHUNK, (r + 1) * CHUNK)
            us[1 - k][:, cut] = dot(tb[1 - k], taug[:, lanes_of(nxt, r)])
            vs[k][:, cut] = values(us[k][:, cut])
            out[prev, :, cut] += dot(skp[k], vs[1 - k][:, cut])
        skp[1 - k] = skt[k]

    ready(0, 0)
    us[0][...] = dot(tb[0], taug[:, pl.ds(pl.multiple_of(unit[0, 0] * half, half), half)])
    skp[0] = jnp.zeros_like(skp[0])
    vs[1][...] = jnp.zeros_like(vs[1])

    def turn(size, start, i, _):
        for k in range(size):
            stage(start + size * i + k, k % 2)
        return 0

    todo = (total + 1) // 2 * 2
    left = jnp.int32(0)
    for size in SIZES:
        many = (todo - left) // size
        lax.fori_loop(0, many, functools.partial(turn, size, left), 0)
        left = left + many * size
    last = unit[0, jnp.maximum(left - 1, 0)]
    out[last] += dot(skp[0], vs[1][...])


def sum_body(dims, shares, part, taug, saug, out, cache, buf,
             s2, r2, s3, a3, r3, low, full, send, recv, sem):
    nx, nz, ny, nc = dims
    me = lax.axis_index("tile")
    x = lax.axis_index("row")
    c = lax.rem(me, nc)
    y = lax.rem(me // nc, ny)
    z = me // (nc * ny)
    n, half = part.shape[1], part.shape[2]
    lanes = half // ny
    kz = n // nz
    panels, width = cache.shape[0], cache.shape[1]
    quarter = half * nc

    def tile_of(zz, yy, cc):
        return (zz * ny + yy) * nc + cc

    core_peer = {"tile": tile_of(z, y, 1 - c)}
    y_peers = [{"tile": tile_of(z, lax.rem(y + o, ny), c)} for o in range(1, ny)]
    z_peers = [{"tile": tile_of(lax.rem(z + o, nz), y, c)} for o in range(1, nz)]
    far = [(ox, oz) for oz in range(nz) for ox in range(nx) if ox or oz]
    xz_peers = [{"row": lax.rem(x + ox, nx), "tile": tile_of(lax.rem(z + oz, nz), y, c)} for ox, oz in far]
    barrier = pltpu.get_barrier_semaphore()
    peers = [core_peer] + y_peers + xz_peers
    for p in peers:
        pl.semaphore_signal(barrier, inc=1, device_id=p, device_id_type=MESH)
    count = [0]

    def push(src, dst, peer):
        k = count[0]
        count[0] += 1
        copy = pltpu.make_async_remote_copy(
            src_ref=src, dst_ref=dst, send_sem=send.at[k], recv_sem=recv.at[k],
            device_id=peer, device_id_type=MESH)
        copy.start()
        return copy

    def keep(i):
        slot = lax.rem(i, 2)
        return pltpu.make_async_copy(buf.at[slot], cache.at[pl.ds(2 * i, 2)], sem.at[slot])

    def step(i, _):
        slot = lax.rem(i, 2)

        @pl.when(i >= 2)
        def _():
            keep(i - 2).wait()

        tb = saug[pl.ds(pl.multiple_of((c * panels + 2 * i) * width, 2 * width), 2 * width)]
        for r in range(nx - 1):
            v = values(dot(tb, taug[:, r * quarter : (r + 1) * quarter]))
            for k in range(2):
                buf[slot, k, :, r * quarter : (r + 1) * quarter] = v[k * width : (k + 1) * width]
        keep(i).start()
        return 0

    edges = [sum(shares[:k]) for k in range(len(shares) + 1)]

    def work(k):
        if edges[k + 1] > edges[k]:
            lax.fori_loop(edges[k], edges[k + 1], step, 0)

    def finish(made):
        for copy in made:
            copy.wait()

    for q in range(ny):
        s2[q] = part[:, :, q * lanes : (q + 1) * lanes].astype(BF16)
    pl.semaphore_wait(barrier, len(peers))
    flight = [push(s2.at[lax.rem(y + o, ny)], r2.at[o - 1], y_peers[o - 1]) for o in range(1, ny)]
    work(0)
    finish(flight)
    at = pl.ds(pl.multiple_of(y * lanes, lanes), lanes)
    for q in range(nz):
        cut = slice(q * kz, (q + 1) * kz)
        a = part[:, cut, at]
        for o in range(1, ny):
            a = a + r2[o - 1, :, cut, :].astype(F32)
        a3[q] = a
        s3[q] = a.astype(BF16)
    flight = [push(s3.at[lax.rem(z + o, nz)], r3.at[o - 1], z_peers[o - 1]) for o in range(1, nz)]
    work(1)
    finish(flight)
    a = a3[z]
    for o in range(1, nz):
        a = a + r3[o - 1].astype(F32)
    low[...] = a.astype(BF16)
    full[c, y, z, x] = low[x]
    flight = [push(low.at[lax.rem(x + ox, nx)], full.at[c, y, z, x], p) for (ox, oz), p in zip(far, xz_peers)]
    work(2)
    finish(flight)
    flight = [push(full.at[c, y], full.at[c, y], p) for p in y_peers]
    near = [push(full.at[c, y], full.at[c, y], core_peer)]
    work(3)
    finish(flight)
    near += [push(full.at[c, lax.rem(y + o, ny)], full.at[c, lax.rem(y + o, ny)], core_peer) for o in range(1, ny)]
    work(4)
    finish(near)
    out[...] = full[...]
    if edges[-1]:
        keep(panels // 2 - 2).wait()
        keep(panels // 2 - 1).wait()


def eliminate(blk, left, right, linv):
    n = left.shape[0]
    at = pl.multiple_of(blk * 8, 8)
    low, inv = left[...], right[...]
    rid = lax.broadcasted_iota(jnp.int32, (n, 1), 0)
    rows, gains = left[pl.ds(at, 8), :], right[pl.ds(at, 8), :]
    r8 = lax.broadcasted_iota(jnp.int32, (8, 1), 0)
    for j in range(8):
        top, gain = rows[j : j + 1], gains[j : j + 1]
        scale = 1.0 / top[:, j : j + 1]
        f8 = jnp.where(r8 > j, rows[:, j : j + 1] * scale, 0.0)
        f = jnp.where(rid >= at + 8, low[:, j : j + 1] * scale, 0.0)
        rows = rows - f8 * top
        gains = gains - f8 * gain
        low = low - f * top
        inv = inv - f * gain
    left[...] = pltpu.roll(low, n - 8, 1)
    right[...] = inv
    lane = lax.broadcasted_iota(jnp.int32, (8, n), 1)
    d = jnp.sum(jnp.where(lane == r8, rows, 0.0), axis=1, keepdims=True)
    linv[pl.ds(at, 8), :] = gains * lax.rsqrt(d)


def dot_full(a, b):
    return jnp.dot(a, b, precision=lax.Precision.HIGHEST, preferred_element_type=F32)


DEPTH = 3


def project_body(flags_hbm, low, taug, saug, cache, basis, proj, flags, st, left, right, linv, z, buf, fsem, sem):
    panels, width = cache.shape[0], cache.shape[1]
    n = proj.shape[0]
    nc, ny, nz, nx, kz, lanes = low.shape
    quarter = nc * ny * lanes
    steps = panels // 2
    x = lax.axis_index("row")
    me = lax.axis_index("tile")
    core = lax.rem(me, nc)

    def in_copy(i):
        slot = lax.rem(i, DEPTH)
        return pltpu.make_async_copy(cache.at[pl.ds(2 * i, 2)], buf.at[slot], sem.at[slot])

    flag_copy = pltpu.make_async_copy(flags_hbm, flags, fsem)
    flag_copy.start()
    for i in range(DEPTH - 1):
        in_copy(i).start()
    for k in range(nx):
        q = lax.rem(x + k, nx)
        for c in range(nc):
            for y in range(ny):
                at = k * quarter + (c * ny + y) * lanes
                st[:, at : at + lanes] = low[c, y, :, q].reshape(n, lanes)
    gram = dot_nt(st[...], st[...])
    ri = lax.broadcasted_iota(jnp.int32, (n, n), 0)
    ci = lax.broadcasted_iota(jnp.int32, (n, n), 1)
    eye = (ri == ci).astype(F32)
    shift = 0.0001 * jnp.sum(gram * eye) / n
    left[...] = gram + shift * eye
    right[...] = eye

    def step(i, _):
        slot = lax.rem(i, DEPTH)

        @pl.when(i + DEPTH - 1 < steps)
        def _():
            in_copy(i + DEPTH - 1).start()

        in_copy(i).wait()
        tb = saug[pl.ds(pl.multiple_of((core * panels + 2 * i) * width, 2 * width), 2 * width)]
        own = values(dot(tb, taug[...]))
        rest = buf[slot].reshape(2 * width, (nx - 1) * quarter)
        o = dot_nt(st[:, quarter:], rest) + dot_nt(st[:, :quarter], own)
        z[:, pl.ds(pl.multiple_of(i * 2 * width, 2 * width), 2 * width)] = o
        eliminate(i, left, right, linv)
        return 0

    lax.fori_loop(0, steps, step, 0)
    flag_copy.wait()
    factor = linv[...]
    own = basis.shape[0]
    per = quarter // own
    k = lax.rem(me // per - x + nx, nx)
    at = pl.multiple_of(k * quarter + lax.rem(me, per) // 2 * 128, 128)
    block = dot_full(factor, st[:, pl.ds(at, 128)].astype(F32)).T
    basis[...] = jnp.where(lax.rem(me, 2) == 0, block[:own], block[own:])
    for g in range(panels):
        cut = slice(g * width, (g + 1) * width)
        o = dot_full(factor, z[:, cut])
        proj[:, cut] = jnp.where(flags[x, core, 0, g] > 0, o, 0.0).astype(BF16)


SHARES = (4, 3, 4, 4, 1)


def sum_call(part, tr, sa, shares):
    nx, n, half = part.shape
    rest = tr.shape[1]
    nc, ny = 2, 4
    nz = lax.axis_size("tile") // (nc * ny)
    lanes = half // ny
    kz = n // nz
    width = 128
    copies = ny + nz + nx * nz + ny
    vmem = pl.BlockSpec(memory_space=pltpu.VMEM)
    hbm = pl.BlockSpec(memory_space=pltpu.HBM)
    dma = pltpu.SemaphoreType.DMA
    VM = pltpu.VMEM
    return pl.pallas_call(
        functools.partial(sum_body, (nx, nz, ny, nc), shares),
        in_specs=[vmem, vmem, vmem],
        out_specs=[vmem, hbm],
        out_shape=[jax.ShapeDtypeStruct((nc, ny, nz, nx, kz, lanes), BF16),
                   jax.ShapeDtypeStruct((sa.shape[0] // nc // width, width, rest), BF16)],
        scratch_shapes=[
            VM((2, 2, width, rest), BF16),
            VM((ny, nx, n, lanes), BF16), VM((ny - 1, nx, n, lanes), BF16),
            VM((nz, nx, kz, lanes), BF16), VM((nz, nx, kz, lanes), F32), VM((nz - 1, nx, kz, lanes), BF16),
            VM((nx, kz, lanes), BF16), VM((nc, ny, nz, nx, kz, lanes), BF16),
            dma((copies,)), dma((copies,)), dma((2,))],
        compiler_params=pltpu.CompilerParams(
            collective_id=0, has_side_effects=True, vmem_limit_bytes=40 << 20),
        name="sum_rows",
    )(part, tr, sa)


def sketch_call(flags, ta, sa, skt):
    blocks = flags.shape[0]
    panels, width, n = skt.shape
    half = ta.shape[1] // blocks
    vmem = pl.BlockSpec(memory_space=pltpu.VMEM)
    hbm = pl.BlockSpec(memory_space=pltpu.HBM)
    VM = pltpu.VMEM
    wide = GROUP * width
    return pl.pallas_call(
        sketch_body,
        in_specs=[hbm, vmem, vmem, vmem],
        out_specs=vmem,
        out_shape=jax.ShapeDtypeStruct((blocks, n, half), F32),
        scratch_shapes=[
            pltpu.SMEM(flags.shape, jnp.int32), pltpu.SMEM((panels + 1,), jnp.int32),
            pltpu.SMEM((GROUP + 1, blocks * panels // GROUP + 2), jnp.int32),
            VM((2, wide, KA), BF16), VM((2, n, wide), BF16), VM((2, n, wide), BF16),
            VM((wide, half), F32), VM((wide, half), F32), VM((wide, half), BF16), VM((wide, half), BF16),
            pltpu.SemaphoreType.DMA],
        compiler_params=pltpu.CompilerParams(vmem_limit_bytes=40 << 20),
        name="sketch",
    )(flags, ta, sa, skt)


def project_call(flags, low, tq, sa, cache, rows, own):
    n = low.shape[2] * low.shape[4]
    panels, width, rest = cache.shape
    cols = panels * width
    vmem = pl.BlockSpec(memory_space=pltpu.VMEM)
    hbm = pl.BlockSpec(memory_space=pltpu.HBM)
    dma = pltpu.SemaphoreType.DMA
    VM = pltpu.VMEM
    return pl.pallas_call(
        project_body,
        in_specs=[hbm, vmem, vmem, vmem, hbm],
        out_specs=[vmem, vmem],
        out_shape=[jax.ShapeDtypeStruct((own, n), F32), jax.ShapeDtypeStruct((n, cols), BF16)],
        scratch_shapes=[
            pltpu.SMEM(flags.shape, jnp.int32),
            VM((n, rows), BF16), VM((n, n), F32), VM((n, n), F32), VM((n, n), F32), VM((n, cols), F32),
            VM((DEPTH, 2, width, rest), BF16), dma, dma((DEPTH,))],
        compiler_params=pltpu.CompilerParams(vmem_limit_bytes=40 << 20),
        name="project",
    )(flags, low, tq, sa, cache)


def prepare_call(admissible, row_points, source_points, sketch, blocks):
    panels = admissible.shape[1]
    cols, n = sketch.shape
    width = cols // panels
    rows = row_points.shape[1] // blocks
    nx, nc = blocks, 2
    quarter = rows // nx
    rest = rows - quarter
    vmem = pl.BlockSpec(memory_space=pltpu.VMEM)
    hbm = pl.BlockSpec(memory_space=pltpu.HBM)
    dma = pltpu.SemaphoreType.DMA
    VM = pltpu.VMEM
    copies = nx * nc + 1
    return pl.pallas_call(
        prepare_body,
        in_specs=[vmem, hbm, hbm, hbm],
        out_specs=[vmem] * 6,
        out_shape=[jax.ShapeDtypeStruct((nx, nc, 8, 128), jnp.int32), jax.ShapeDtypeStruct((KA, rows // nc), BF16),
                   jax.ShapeDtypeStruct((KA, rest), BF16), jax.ShapeDtypeStruct((KA, quarter), BF16),
                   jax.ShapeDtypeStruct((nc * cols, KA), BF16),
                   jax.ShapeDtypeStruct((nc * panels, n, width), BF16)],
        scratch_shapes=[
            VM((3, rows // nc), F32), VM((3, rows), F32), VM((3, cols), F32), VM((cols, n), BF16),
            VM((KA, max(rows, cols)), F32), VM((8, 128), jnp.int32), VM((nx, nc, 8, 128), jnp.int32),
            VM((cols, KA), BF16), VM((panels, n, width), BF16),
            dma((copies,)), dma((copies,)), dma((2 * nx + 2,))],
        compiler_params=pltpu.CompilerParams(
            collective_id=1, has_side_effects=True, vmem_limit_bytes=24 << 20),
        name="prepare",
    )(admissible, row_points, source_points, sketch)


def local(row_points, source_points, sketch, admissible):
    blocks = lax.axis_size("row")
    rows = row_points.shape[1] // blocks
    own = rows // lax.axis_size("tile")
    flags, ta, tr, tq, sa, skt = prepare_call(admissible, row_points, source_points, sketch, blocks)
    part = sketch_call(flags, ta, sa, skt)
    low, cache = sum_call(part, tr, sa, SHARES)
    basis, proj = project_call(flags, low, tq, sa, cache, rows, own)
    return (basis, proj[None])


def solution(mesh):
    in_specs = (P(), P(None, "tile"), P("tile", None), P("row", "tile"))
    out_specs = (P(("row", "tile"), None), P("row", None, "tile"))
    return jax.shard_map(local, mesh=mesh, in_specs=in_specs, out_specs=out_specs, check_vma=False)
```

```python
import functools
import math

import jax
import jax.numpy as jnp
from jax import lax
from jax.experimental import pallas as pl
from jax.experimental.pallas import tpu as pltpu
from jax.sharding import PartitionSpec as P

DAMPING = 0.25
WAVENUM = 24.0
TURN = WAVENUM / (2.0 * math.pi)
DECAY = -DAMPING * math.log2(math.e) / TURN
SCALE = TURN / (4.0 * math.pi)
HALF_TURN = (0.9999982891022392, -4.934458900946806, 4.048771386943898, -1.2477978368551703)
COEFS = tuple(c * math.sqrt(2.0 * SCALE) for c in HALF_TURN)
F32 = jnp.float32
BF16 = jnp.bfloat16
MESH = pl.DeviceIdType.MESH

KA = 32
CHUNK = 256
SIZES = (4, 2)
GROUP = 4


def dot(a, b):
    return jnp.dot(a, b, preferred_element_type=F32)


def dot_nt(a, b):
    return lax.dot_general(a, b, (((1,), (1,)), ((), ())), preferred_element_type=F32)


def values(u):
    rs = lax.rsqrt(u)
    t = u * rs
    f = t - jnp.round(t)
    y = f * f
    c = ((COEFS[3] * y + COEFS[2]) * y + COEFS[1]) * y + COEFS[0]
    amp = jnp.exp2(t * DECAY) * rs
    return (amp * (c * c - SCALE)).astype(BF16)


def split3(x):
    hi = x.astype(BF16).astype(F32)
    rem = x - hi
    mid = rem.astype(BF16).astype(F32)
    return hi, mid, rem - mid


def put_aug(tmp, ref, pts, is_source):
    fill_aug(tmp, pts, is_source)
    ref[...] = tmp[...].astype(BF16)


def fill_aug(tmp, pts, is_source):
    n = pts.shape[1]
    x = (pts[0:1] - 3.0) * TURN
    y = (pts[1:2] - 3.0) * TURN
    z = (pts[2:3] + 1.1) * TURN
    norm = list(split3(x * x + y * y + z * z))
    rows = []
    for v in (x, y, z):
        hi, mid, lo = split3(v)
        if is_source:
            hi, mid, lo = -2.0 * hi, -2.0 * mid, -2.0 * lo
            rows += [hi, mid, hi, mid, lo, hi]
        else:
            rows += [hi, hi, mid, mid, hi, lo]
    ones = [jnp.ones((1, n), F32)] * 3
    rows += ones + norm if is_source else norm + ones
    for r, v in enumerate(rows):
        tmp[r : r + 1, :] = v
    tmp[len(rows) :, :] = jnp.zeros((KA - len(rows), n), F32)


def prepare_body(flags_hbm, tpts_hbm, spts_hbm, sk_hbm, flags, ta, tr, tq, sa, skt,
                 own_flags, tpts, trest, spts, sk, tmp, stage, got, far_spts, sk_got, send, recv, insem):
    nx, nc = flags.shape[0], flags.shape[1]
    x = lax.axis_index("row")
    me = lax.axis_index("tile")
    c = lax.rem(me, nc)
    half = ta.shape[1] // nx
    quarter = half * nc
    rows = nx * quarter
    panels, width = skt.shape[0] // nc, skt.shape[1]

    def piece(b, at, size, dst, k):
        at = pl.multiple_of(b * rows + at, size)
        return pltpu.make_async_copy(tpts_hbm.at[:, pl.ds(at, size)], dst, insem.at[k])

    copies = [piece(b, x * quarter + c * half, half, tpts.at[:, b * half : (b + 1) * half], b) for b in range(nx)]
    copies += [piece(x, lax.rem(x + k, nx) * quarter, quarter, trest.at[:, k * quarter : (k + 1) * quarter], nx + k)
               for k in range(nx)]
    copies.append(pltpu.make_async_copy(spts_hbm, spts, insem.at[2 * nx]))
    copies.append(pltpu.make_async_copy(sk_hbm, sk, insem.at[2 * nx + 1]))
    flag_copy = pltpu.make_async_copy(flags_hbm, own_flags, insem.at[2 * nx + 2])
    flag_copy.start()
    for copy in copies[2 * nx :] + copies[: 2 * nx]:
        copy.start()
    barrier = pltpu.get_barrier_semaphore()
    peers = [(o, k) for o in range(nx) for k in range(nc) if o or k]

    def device(o, k):
        return {"row": lax.rem(x + o, nx), "tile": me - c + lax.rem(c + k, nc)}

    for p in peers:
        pl.semaphore_signal(barrier, inc=1, device_id=device(*p), device_id_type=MESH)
    stage[...] = jnp.zeros_like(stage)
    flag_copy.wait()
    stage[0:1, 0 : own_flags.shape[1]] = own_flags[...]
    got[x, c] = stage[...]
    flight = []

    def push(src, dst, p):
        n = len(flight)
        copy = pltpu.make_async_remote_copy(
            src_ref=src, dst_ref=dst, send_sem=send.at[n], recv_sem=recv.at[n],
            device_id=device(*p), device_id_type=MESH)
        copy.start()
        flight.append(copy)

    pl.semaphore_wait(barrier, len(peers))
    for p in peers:
        push(stage, got.at[x, c], p)
    copies[2 * nx].wait()
    push(spts, far_spts, (0, 1))
    copies[2 * nx + 1].wait()
    cols = panels * width

    def turn_sketch(i, _):
        at = pl.ds(pl.multiple_of(i * width, width), width)
        skt[c * panels + i] = sk[at, :].astype(F32).T.astype(BF16)
        return 0

    lax.fori_loop(0, panels, turn_sketch, 0, unroll=4)
    push(skt.at[pl.ds(c * panels, panels)], sk_got, (0, 1))

    def turn_sources(core, i, _):
        at = pl.ds(pl.multiple_of(i * width, width), width)
        sa[pl.ds(pl.multiple_of(core * cols + i * width, width), width), :] = tmp[:, at].T.astype(BF16)
        return 0

    fill_aug(tmp, spts[...], True)
    lax.fori_loop(0, panels, functools.partial(turn_sources, c), 0, unroll=4)
    for copy in copies[: 2 * nx]:
        copy.wait()
    put_aug(tmp.at[:, : ta.shape[1]], ta, tpts[...], False)
    fill_aug(tmp, trest[...], False)
    tq[...] = tmp[:, :quarter].astype(BF16)
    tr[...] = tmp[:, quarter:].astype(BF16)
    for copy in flight[:-1]:
        copy.wait()
    flags[...] = got[...]
    fill_aug(tmp, far_spts[...], True)
    lax.fori_loop(0, panels, functools.partial(turn_sources, 1 - c), 0, unroll=4)
    flight[-1].wait()
    skt[pl.ds((1 - c) * panels, panels)] = sk_got[...]


def sketch_body(flags_hbm, taug, saug, skta, out, flags, order, unit, tb, skt, skp, u0, u1, v0, v1, insem):
    us, vs = (u0, u1), (v0, v1)
    blocks, n, half = out.shape
    nc = flags.shape[1]
    panels, width = skta.shape[0], skta.shape[1]
    per = panels // nc

    flag_copy = pltpu.make_async_copy(flags_hbm, flags, insem)
    flag_copy.start()
    out[...] = jnp.zeros_like(out)
    flag_copy.wait()
    total = jnp.int32(0)
    for b in range(blocks):

        count = jnp.int32(0)
        for core in range(nc):

            def note(i, count, b=b, core=core):
                for k in range(8):
                    order[count] = core * per + 8 * i + k
                    count = count + flags[b, core, 0, 8 * i + k]
                return count

            count = lax.fori_loop(0, per // 8, note, count)

        def put(i, at, b=b, count=count):
            unit[0, at] = b
            for h in range(GROUP):
                k = GROUP * i + h
                unit[1 + h, at] = jnp.where(k < count, order[jnp.minimum(k, panels)], panels)
            return at + 1

        total = lax.fori_loop(0, (count + GROUP - 1) // GROUP, put, total)
    for k in range(2):
        for h in range(GROUP + 1):
            unit[h, total + k] = panels if h else 0

    def ready(at, k):
        for h in range(GROUP):
            g = unit[1 + h, at]
            mark = jnp.where(g < panels, 1.0, 0.0).astype(BF16)
            g = jnp.minimum(g, panels - 1)
            part = slice(h * width, (h + 1) * width)
            tb[k, part, :] = saug[pl.ds(pl.multiple_of(g * width, width), width), :]
            skt[k, :, part] = skta[g] * mark

    def lanes_of(b, r):
        return pl.ds(pl.multiple_of(b * half + r * CHUNK, CHUNK), CHUNK)

    def stage(at, k):
        prev, nxt = unit[0, jnp.maximum(at - 1, 0)], unit[0, at + 1]
        ready(at + 1, 1 - k)
        for r in range(half // CHUNK):
            cut = slice(r * CHUNK, (r + 1) * CHUNK)
            us[1 - k][:, cut] = dot(tb[1 - k], taug[:, lanes_of(nxt, r)])
            vs[k][:, cut] = values(us[k][:, cut])
            out[prev, :, cut] += dot(skp[k], vs[1 - k][:, cut])
        skp[1 - k] = skt[k]

    ready(0, 0)
    us[0][...] = dot(tb[0], taug[:, pl.ds(pl.multiple_of(unit[0, 0] * half, half), half)])
    skp[0] = jnp.zeros_like(skp[0])
    vs[1][...] = jnp.zeros_like(vs[1])

    def turn(size, start, i, _):
        for k in range(size):
            stage(start + size * i + k, k % 2)
        return 0

    todo = (total + 1) // 2 * 2
    left = jnp.int32(0)
    for size in SIZES:
        many = (todo - left) // size
        lax.fori_loop(0, many, functools.partial(turn, size, left), 0)
        left = left + many * size
    last = unit[0, jnp.maximum(left - 1, 0)]
    out[last] += dot(skp[0], vs[1][...])


def sum_body(dims, shares, part, taug, saug, out, cache, buf,
             s2, r2, s3, a3, r3, low, full, send, recv, sem):
    nx, nz, ny, nc = dims
    me = lax.axis_index("tile")
    x = lax.axis_index("row")
    c = lax.rem(me, nc)
    y = lax.rem(me // nc, ny)
    z = me // (nc * ny)
    n, half = part.shape[1], part.shape[2]
    lanes = half // ny
    kz = n // nz
    panels, width = cache.shape[0], cache.shape[1]
    quarter = half * nc

    def tile_of(zz, yy, cc):
        return (zz * ny + yy) * nc + cc

    core_peer = {"tile": tile_of(z, y, 1 - c)}
    y_peers = [{"tile": tile_of(z, lax.rem(y + o, ny), c)} for o in range(1, ny)]
    z_peers = [{"tile": tile_of(lax.rem(z + o, nz), y, c)} for o in range(1, nz)]
    far = [(ox, oz) for oz in range(nz) for ox in range(nx) if ox or oz]
    xz_peers = [{"row": lax.rem(x + ox, nx), "tile": tile_of(lax.rem(z + oz, nz), y, c)} for ox, oz in far]
    barrier = pltpu.get_barrier_semaphore()
    peers = [core_peer] + y_peers + xz_peers
    for p in peers:
        pl.semaphore_signal(barrier, inc=1, device_id=p, device_id_type=MESH)
    count = [0]

    def push(src, dst, peer):
        k = count[0]
        count[0] += 1
        copy = pltpu.make_async_remote_copy(
            src_ref=src, dst_ref=dst, send_sem=send.at[k], recv_sem=recv.at[k],
            device_id=peer, device_id_type=MESH)
        copy.start()
        return copy

    def keep(i):
        slot = lax.rem(i, 2)
        return pltpu.make_async_copy(buf.at[slot], cache.at[pl.ds(2 * i, 2)], sem.at[slot])

    def step(i, _):
        slot = lax.rem(i, 2)

        @pl.when(i >= 2)
        def _():
            keep(i - 2).wait()

        tb = saug[pl.ds(pl.multiple_of((c * panels + 2 * i) * width, 2 * width), 2 * width)]
        for r in range(nx - 1):
            v = values(dot(tb, taug[:, r * quarter : (r + 1) * quarter]))
            for k in range(2):
                buf[slot, k, :, r * quarter : (r + 1) * quarter] = v[k * width : (k + 1) * width]
        keep(i).start()
        return 0

    edges = [sum(shares[:k]) for k in range(len(shares) + 1)]

    def work(k):
        if edges[k + 1] > edges[k]:
            lax.fori_loop(edges[k], edges[k + 1], step, 0)

    def finish(made):
        for copy in made:
            copy.wait()

    for q in range(ny):
        s2[q] = part[:, :, q * lanes : (q + 1) * lanes].astype(BF16)
    pl.semaphore_wait(barrier, len(peers))
    flight = [push(s2.at[lax.rem(y + o, ny)], r2.at[o - 1], y_peers[o - 1]) for o in range(1, ny)]
    work(0)
    finish(flight)
    at = pl.ds(pl.multiple_of(y * lanes, lanes), lanes)
    for q in range(nz):
        cut = slice(q * kz, (q + 1) * kz)
        a = part[:, cut, at]
        for o in range(1, ny):
            a = a + r2[o - 1, :, cut, :].astype(F32)
        a3[q] = a
        s3[q] = a.astype(BF16)
    flight = [push(s3.at[lax.rem(z + o, nz)], r3.at[o - 1], z_peers[o - 1]) for o in range(1, nz)]
    work(1)
    finish(flight)
    a = a3[z]
    for o in range(1, nz):
        a = a + r3[o - 1].astype(F32)
    low[...] = a.astype(BF16)
    full[c, y, z, x] = low[x]
    flight = [push(low.at[lax.rem(x + ox, nx)], full.at[c, y, z, x], p) for (ox, oz), p in zip(far, xz_peers)]
    work(2)
    finish(flight)
    flight = [push(full.at[c, y], full.at[c, y], p) for p in y_peers]
    near = [push(full.at[c, y], full.at[c, y], core_peer)]
    work(3)
    finish(flight)
    near += [push(full.at[c, lax.rem(y + o, ny)], full.at[c, lax.rem(y + o, ny)], core_peer) for o in range(1, ny)]
    work(4)
    finish(near)
    out[...] = full[...]
    if edges[-1]:
        keep(panels // 2 - 2).wait()
        keep(panels // 2 - 1).wait()


def eliminate(blk, left, right, linv):
    n = left.shape[0]
    at = pl.multiple_of(blk * 8, 8)
    low, inv = left[...], right[...]
    rid = lax.broadcasted_iota(jnp.int32, (n, 1), 0)
    rows, gains = left[pl.ds(at, 8), :], right[pl.ds(at, 8), :]
    r8 = lax.broadcasted_iota(jnp.int32, (8, 1), 0)
    for j in range(8):
        top, gain = rows[j : j + 1], gains[j : j + 1]
        scale = 1.0 / top[:, j : j + 1]
        f8 = jnp.where(r8 > j, rows[:, j : j + 1] * scale, 0.0)
        f = jnp.where(rid >= at + 8, low[:, j : j + 1] * scale, 0.0)
        rows = rows - f8 * top
        gains = gains - f8 * gain
        low = low - f * top
        inv = inv - f * gain
    left[...] = pltpu.roll(low, n - 8, 1)
    right[...] = inv
    lane = lax.broadcasted_iota(jnp.int32, (8, n), 1)
    d = jnp.sum(jnp.where(lane == r8, rows, 0.0), axis=1, keepdims=True)
    linv[pl.ds(at, 8), :] = gains * lax.rsqrt(d)


def dot_full(a, b):
    return jnp.dot(a, b, precision=lax.Precision.HIGHEST, preferred_element_type=F32)


DEPTH = 3


def project_body(flags_hbm, low, taug, saug, cache, basis, proj, flags, st, left, right, linv, z, buf, fsem, sem):
    panels, width = cache.shape[0], cache.shape[1]
    n = proj.shape[0]
    nc, ny, nz, nx, kz, lanes = low.shape
    quarter = nc * ny * lanes
    steps = panels // 2
    x = lax.axis_index("row")
    me = lax.axis_index("tile")
    core = lax.rem(me, nc)

    def in_copy(i):
        slot = lax.rem(i, DEPTH)
        return pltpu.make_async_copy(cache.at[pl.ds(2 * i, 2)], buf.at[slot], sem.at[slot])

    flag_copy = pltpu.make_async_copy(flags_hbm, flags, fsem)
    flag_copy.start()
    for i in range(DEPTH - 1):
        in_copy(i).start()
    for k in range(nx):
        q = lax.rem(x + k, nx)
        for c in range(nc):
            for y in range(ny):
                at = k * quarter + (c * ny + y) * lanes
                st[:, at : at + lanes] = low[c, y, :, q].reshape(n, lanes)
    gram = dot_nt(st[...], st[...])
    ri = lax.broadcasted_iota(jnp.int32, (n, n), 0)
    ci = lax.broadcasted_iota(jnp.int32, (n, n), 1)
    eye = (ri == ci).astype(F32)
    shift = 0.0001 * jnp.sum(gram * eye) / n
    left[...] = gram + shift * eye
    right[...] = eye

    def step(i, _):
        slot = lax.rem(i, DEPTH)

        @pl.when(i + DEPTH - 1 < steps)
        def _():
            in_copy(i + DEPTH - 1).start()

        in_copy(i).wait()
        tb = saug[pl.ds(pl.multiple_of((core * panels + 2 * i) * width, 2 * width), 2 * width)]
        own = values(dot(tb, taug[...]))
        rest = buf[slot].reshape(2 * width, (nx - 1) * quarter)
        o = dot_nt(st[:, quarter:], rest) + dot_nt(st[:, :quarter], own)
        z[:, pl.ds(pl.multiple_of(i * 2 * width, 2 * width), 2 * width)] = o
        eliminate(i, left, right, linv)
        return 0

    lax.fori_loop(0, steps, step, 0)
    flag_copy.wait()
    factor = linv[...]
    own = basis.shape[0]
    per = quarter // own
    k = lax.rem(me // per - x + nx, nx)
    at = pl.multiple_of(k * quarter + lax.rem(me, per) // 2 * 128, 128)
    block = dot_full(factor, st[:, pl.ds(at, 128)].astype(F32)).T
    basis[...] = jnp.where(lax.rem(me, 2) == 0, block[:own], block[own:])
    for w in range(0, panels, 8):
        o = dot_full(factor, z[:, w * width : (w + 8) * width])
        for g in range(w, w + 8):
            part = o[:, (g - w) * width : (g - w + 1) * width]
            proj[:, g * width : (g + 1) * width] = jnp.where(flags[x, core, 0, g] > 0, part, 0.0).astype(BF16)


SHARES = (4, 3, 4, 4, 1)


def sum_call(part, tr, sa, shares):
    nx, n, half = part.shape
    rest = tr.shape[1]
    nc, ny = 2, 4
    nz = lax.axis_size("tile") // (nc * ny)
    lanes = half // ny
    kz = n // nz
    width = 128
    copies = ny + nz + nx * nz + ny
    vmem = pl.BlockSpec(memory_space=pltpu.VMEM)
    hbm = pl.BlockSpec(memory_space=pltpu.HBM)
    dma = pltpu.SemaphoreType.DMA
    VM = pltpu.VMEM
    return pl.pallas_call(
        functools.partial(sum_body, (nx, nz, ny, nc), shares),
        in_specs=[vmem, vmem, vmem],
        out_specs=[vmem, hbm],
        out_shape=[jax.ShapeDtypeStruct((nc, ny, nz, nx, kz, lanes), BF16),
                   jax.ShapeDtypeStruct((sa.shape[0] // nc // width, width, rest), BF16)],
        scratch_shapes=[
            VM((2, 2, width, rest), BF16),
            VM((ny, nx, n, lanes), BF16), VM((ny - 1, nx, n, lanes), BF16),
            VM((nz, nx, kz, lanes), BF16), VM((nz, nx, kz, lanes), F32), VM((nz - 1, nx, kz, lanes), BF16),
            VM((nx, kz, lanes), BF16), VM((nc, ny, nz, nx, kz, lanes), BF16),
            dma((copies,)), dma((copies,)), dma((2,))],
        compiler_params=pltpu.CompilerParams(
            collective_id=0, has_side_effects=True, vmem_limit_bytes=40 << 20),
        name="sum_rows",
    )(part, tr, sa)


def sketch_call(flags, ta, sa, skt):
    blocks = flags.shape[0]
    panels, width, n = skt.shape
    half = ta.shape[1] // blocks
    vmem = pl.BlockSpec(memory_space=pltpu.VMEM)
    hbm = pl.BlockSpec(memory_space=pltpu.HBM)
    VM = pltpu.VMEM
    wide = GROUP * width
    return pl.pallas_call(
        sketch_body,
        in_specs=[hbm, vmem, vmem, vmem],
        out_specs=vmem,
        out_shape=jax.ShapeDtypeStruct((blocks, n, half), F32),
        scratch_shapes=[
            pltpu.SMEM(flags.shape, jnp.int32), pltpu.SMEM((panels + 1,), jnp.int32),
            pltpu.SMEM((GROUP + 1, blocks * panels // GROUP + 2), jnp.int32),
            VM((2, wide, KA), BF16), VM((2, n, wide), BF16), VM((2, n, wide), BF16),
            VM((wide, half), F32), VM((wide, half), F32), VM((wide, half), BF16), VM((wide, half), BF16),
            pltpu.SemaphoreType.DMA],
        compiler_params=pltpu.CompilerParams(vmem_limit_bytes=40 << 20),
        name="sketch",
    )(flags, ta, sa, skt)


def project_call(flags, low, tq, sa, cache, rows, own):
    n = low.shape[2] * low.shape[4]
    panels, width, rest = cache.shape
    cols = panels * width
    vmem = pl.BlockSpec(memory_space=pltpu.VMEM)
    hbm = pl.BlockSpec(memory_space=pltpu.HBM)
    dma = pltpu.SemaphoreType.DMA
    VM = pltpu.VMEM
    return pl.pallas_call(
        project_body,
        in_specs=[hbm, vmem, vmem, vmem, hbm],
        out_specs=[vmem, vmem],
        out_shape=[jax.ShapeDtypeStruct((own, n), F32), jax.ShapeDtypeStruct((n, cols), BF16)],
        scratch_shapes=[
            pltpu.SMEM(flags.shape, jnp.int32),
            VM((n, rows), BF16), VM((n, n), F32), VM((n, n), F32), VM((n, n), F32), VM((n, cols), F32),
            VM((DEPTH, 2, width, rest), BF16), dma, dma((DEPTH,))],
        compiler_params=pltpu.CompilerParams(vmem_limit_bytes=40 << 20),
        name="project",
    )(flags, low, tq, sa, cache)


def prepare_call(admissible, row_points, source_points, sketch, blocks):
    panels = admissible.shape[1]
    cols, n = sketch.shape
    width = cols // panels
    rows = row_points.shape[1] // blocks
    nx, nc = blocks, 2
    quarter = rows // nx
    rest = rows - quarter
    vmem = pl.BlockSpec(memory_space=pltpu.VMEM)
    hbm = pl.BlockSpec(memory_space=pltpu.HBM)
    dma = pltpu.SemaphoreType.DMA
    VM = pltpu.VMEM
    copies = nx * nc + 1
    return pl.pallas_call(
        prepare_body,
        in_specs=[hbm] * 4,
        out_specs=[vmem] * 6,
        out_shape=[jax.ShapeDtypeStruct((nx, nc, 8, 128), jnp.int32), jax.ShapeDtypeStruct((KA, rows // nc), BF16),
                   jax.ShapeDtypeStruct((KA, rest), BF16), jax.ShapeDtypeStruct((KA, quarter), BF16),
                   jax.ShapeDtypeStruct((nc * cols, KA), BF16),
                   jax.ShapeDtypeStruct((nc * panels, n, width), BF16)],
        scratch_shapes=[
            VM((1, panels), jnp.int32),
            VM((3, rows // nc), F32), VM((3, rows), F32), VM((3, cols), F32), VM((cols, n), BF16),
            VM((KA, max(rows, cols)), F32), VM((8, 128), jnp.int32), VM((nx, nc, 8, 128), jnp.int32),
            VM((3, cols), F32), VM((panels, n, width), BF16),
            dma((copies,)), dma((copies,)), dma((2 * nx + 3,))],
        compiler_params=pltpu.CompilerParams(
            collective_id=1, has_side_effects=True, vmem_limit_bytes=24 << 20),
        name="prepare",
    )(*[pltpu.with_memory_space_constraint(v, pltpu.HBM)
        for v in (admissible, row_points, source_points, sketch)])


def local(row_points, source_points, sketch, admissible):
    blocks = lax.axis_size("row")
    rows = row_points.shape[1] // blocks
    own = rows // lax.axis_size("tile")
    flags, ta, tr, tq, sa, skt = prepare_call(admissible, row_points, source_points, sketch, blocks)
    part = sketch_call(flags, ta, sa, skt)
    low, cache = sum_call(part, tr, sa, SHARES)
    basis, proj = project_call(flags, low, tq, sa, cache, rows, own)
    return (basis, proj[None])


def solution(mesh):
    in_specs = (P(), P(None, "tile"), P("tile", None), P("row", "tile"))
    out_specs = (P(("row", "tile"), None), P("row", None, "tile"))
    return jax.shard_map(local, mesh=mesh, in_specs=in_specs, out_specs=out_specs, check_vma=False)
```

```python
import functools
import math

import jax
import jax.numpy as jnp
from jax import lax
from jax.experimental import pallas as pl
from jax.experimental.pallas import tpu as pltpu
from jax.sharding import PartitionSpec as P

DAMPING = 0.25
WAVENUM = 24.0
TURN = WAVENUM / (2.0 * math.pi)
DECAY = -DAMPING * math.log2(math.e) / TURN
SCALE = TURN / (4.0 * math.pi)
HALF_TURN = (0.9999982891022392, -4.934458900946806, 4.048771386943898, -1.2477978368551703)
COEFS = tuple(c * math.sqrt(2.0 * SCALE) for c in HALF_TURN)
F32 = jnp.float32
BF16 = jnp.bfloat16
MESH = pl.DeviceIdType.MESH

KA = 32
CHUNK = 256
SIZES = (4, 2)


def dot(a, b):
    return jnp.dot(a, b, preferred_element_type=F32)


def dot_nt(a, b):
    return lax.dot_general(a, b, (((1,), (1,)), ((), ())), preferred_element_type=F32)


def values(u):
    rs = lax.rsqrt(u)
    t = u * rs
    f = t - jnp.round(t)
    y = f * f
    c = ((COEFS[3] * y + COEFS[2]) * y + COEFS[1]) * y + COEFS[0]
    amp = jnp.exp2(t * DECAY) * rs
    return (amp * (c * c - SCALE)).astype(BF16)


def split3(x):
    hi = x.astype(BF16).astype(F32)
    rem = x - hi
    mid = rem.astype(BF16).astype(F32)
    return hi, mid, rem - mid


def put_aug(tmp, ref, pts, is_source):
    fill_aug(tmp, pts, is_source)
    ref[...] = tmp[...].astype(BF16)


def fill_aug(tmp, pts, is_source):
    n = pts.shape[1]
    x = (pts[0:1] - 3.0) * TURN
    y = (pts[1:2] - 3.0) * TURN
    z = (pts[2:3] + 1.1) * TURN
    norm = list(split3(x * x + y * y + z * z))
    rows = []
    for v in (x, y, z):
        hi, mid, lo = split3(v)
        if is_source:
            hi, mid, lo = -2.0 * hi, -2.0 * mid, -2.0 * lo
            rows += [hi, mid, hi, mid, lo, hi]
        else:
            rows += [hi, hi, mid, mid, hi, lo]
    ones = [jnp.ones((1, n), F32)] * 3
    rows += ones + norm if is_source else norm + ones
    for r, v in enumerate(rows):
        tmp[r : r + 1, :] = v
    tmp[len(rows) :, :] = jnp.zeros((KA - len(rows), n), F32)


def compact(flags, row, order, panels):
    def step(i, count):
        for k in range(8):
            order[row, count] = 8 * i + k
            count = count + flags[row, 0, 8 * i + k]
        return count

    return lax.fori_loop(0, panels // 8, step, jnp.int32(0))


def prepare_body(flags_hbm, tpts_hbm, spts_hbm, sk_hbm, flags, ta, tr, sa, skt, own_flags, tpts, trest, spts, sk, tmp, stage, got,
                 send, recv, insem):
    nx = flags.shape[0]
    x = lax.axis_index("row")
    quarter = ta.shape[1] // nx
    rows = nx * quarter

    def piece(b, q, dst, k):
        at = pl.multiple_of(b * rows + q * quarter, quarter)
        return pltpu.make_async_copy(tpts_hbm.at[:, pl.ds(at, quarter)], dst, insem.at[k])

    copies = [piece(b, x, tpts.at[:, b * quarter : (b + 1) * quarter], b) for b in range(nx)]
    copies += [piece(x, lax.rem(x + k, nx), trest.at[:, (k - 1) * quarter : k * quarter], nx + k - 1)
               for k in range(1, nx)]
    copies.append(pltpu.make_async_copy(spts_hbm, spts, insem.at[2 * nx - 1]))
    copies.append(pltpu.make_async_copy(sk_hbm, sk, insem.at[2 * nx]))
    flag_copy = pltpu.make_async_copy(flags_hbm, own_flags, insem.at[2 * nx + 1])
    flag_copy.start()
    for copy in copies:
        copy.start()
    stage[...] = jnp.zeros_like(stage)
    flag_copy.wait()
    stage[0:1, 0 : own_flags.shape[1]] = own_flags[...]
    got[x] = stage[...]
    barrier = pltpu.get_barrier_semaphore()
    peers = [{"row": lax.rem(x + o, nx)} for o in range(1, nx)]
    for p in peers:
        pl.semaphore_signal(barrier, inc=1, device_id=p, device_id_type=MESH)
    pl.semaphore_wait(barrier, len(peers))
    flight = []
    for o, p in enumerate(peers):
        copy = pltpu.make_async_remote_copy(
            src_ref=stage, dst_ref=got.at[x], send_sem=send.at[o], recv_sem=recv.at[o],
            device_id=p, device_id_type=MESH)
        copy.start()
        flight.append(copy)
    for copy in copies[:-1]:
        copy.wait()
    put_aug(tmp, ta, tpts[...], False)
    put_aug(tmp.at[:, : tr.shape[1]], tr, trest[...], False)
    fill_aug(tmp, spts[...], True)
    copies[-1].wait()

    def turn(i, _):
        at = pl.ds(pl.multiple_of(i * 128, 128), 128)
        sa[at, :] = tmp[:, at].T.astype(BF16)
        skt[:, at] = sk[at, :].astype(F32).T.astype(BF16)
        return 0

    lax.fori_loop(0, sk.shape[0] // 128, turn, 0, unroll=4)
    for copy in flight:
        copy.wait()
    flags[...] = got[...]


def sketch_body(flags_hbm, taug, saug, skta, out, cache, flags, order, unit, tb, skt, skp, u0, u1, v0, v1, buf, insem, sem):
    us, vs = (u0, u1), (v0, v1)
    blocks, n, quarter = out.shape
    panels = order.shape[1] - 1
    width = saug.shape[0] // panels
    x = lax.axis_index("row")

    flag_copy = pltpu.make_async_copy(flags_hbm, flags, insem)
    flag_copy.start()
    out[...] = jnp.zeros_like(out)
    flag_copy.wait()
    total = jnp.int32(0)
    own = jnp.int32(0)
    for k in range(blocks):
        b = lax.rem(x + k, blocks)
        count = compact(flags, b, order, panels)
        pairs = (count + 1) // 2

        def put(i, at, b=b, count=count):
            unit[0, at] = b
            unit[1, at] = order[b, 2 * i]
            unit[2, at] = jnp.where(2 * i + 1 < count, order[b, 2 * i + 1], panels)
            return at + 1

        total = lax.fori_loop(0, pairs, put, total)
        if k == 0:
            own = total
    for k in range(5):
        unit[0, total + k] = x
        unit[1, total + k] = panels
        unit[2, total + k] = panels

    def ready(at, k):
        for h in range(2):
            g = unit[1 + h, at]
            mark = jnp.where(g < panels, 1.0, 0.0).astype(BF16)
            col = pl.multiple_of(jnp.minimum(g, panels - 1) * width, width)
            part = slice(h * width, (h + 1) * width)
            tb[k, part, :] = saug[pl.ds(col, width), :]
            skt[k, :, part] = skta[:, pl.ds(col, width)] * mark

    def lanes_of(b, r):
        return pl.ds(pl.multiple_of(b * quarter + r * CHUNK, CHUNK), CHUNK)

    def stage(at, k, own_part=False):
        prev, nxt = unit[0, jnp.maximum(at - 1, 0)], unit[0, at + 1]
        ready(at + 1, 1 - k)
        for r in range(quarter // CHUNK):
            cut = slice(r * CHUNK, (r + 1) * CHUNK)
            us[1 - k][:, cut] = dot(tb[1 - k], taug[:, lanes_of(nxt, r)])
            v = values(us[k][:, cut])
            vs[k][:, cut] = v
            if own_part:
                buf[at, :, cut] = v
            out[prev, :, cut] += dot(skp[k], vs[1 - k][:, cut])
        skp[1 - k] = skt[k]

    def keep(i, k):
        g = unit[1 + k, i]
        return (i < own) & (g < panels), pltpu.make_async_copy(
            buf.at[i, k * width : (k + 1) * width], cache.at[jnp.minimum(g, panels - 1)], sem.at[i, k])

    ready(0, 0)
    us[0][...] = dot(tb[0], taug[:, pl.ds(pl.multiple_of(unit[0, 0] * quarter, quarter), quarter)])
    skp[0] = jnp.zeros_like(skp[0])
    vs[1][...] = jnp.zeros_like(vs[1])

    def own_step(i, _):
        for k in range(4):
            stage(4 * i + k, k % 2, True)
        for k in range(4):
            for h in range(2):
                live, copy = keep(4 * i + k, h)
                pl.when(live)(copy.start)
        return 0

    def other_step(size, start, i, _):
        for k in range(size):
            stage(start + size * i + k, k % 2)
        return 0

    turns = (total + 1) // 2
    own_turns = jnp.minimum((own + 3) // 4, (total + 3) // 4)
    lax.fori_loop(0, own_turns, own_step, 0)
    left = 4 * own_turns
    for size in SIZES:
        many = jnp.maximum(2 * turns - left, 0) // size
        lax.fori_loop(0, many, functools.partial(other_step, size, left), 0)
        left = left + many * size
    last = unit[0, jnp.maximum(left - 1, 0)]
    out[last] += dot(skp[0], vs[1][...])

    def done(i, _):
        for k in range(2):
            live, copy = keep(i, k)
            pl.when(live)(copy.wait)
        return 0

    lax.fori_loop(0, own, done, 0)


def sum_body(dims, shares, part, taug, saug, out, cache, buf,
             s1, r1, a1, s2, r2, s3, a3, r3, low, full, send, recv, sem):
    nx, nz, ny, nc = dims
    me = lax.axis_index("tile")
    x = lax.axis_index("row")
    c = lax.rem(me, nc)
    y = lax.rem(me // nc, ny)
    z = me // (nc * ny)
    n, quarter = part.shape[1], part.shape[2]
    half = quarter // nc
    lanes = half // ny
    kz = n // nz

    def tile_of(zz, yy, cc):
        return {"tile": (zz * ny + yy) * nc + cc}

    core_peer = tile_of(z, y, 1 - c)
    y_peers = [tile_of(z, lax.rem(y + o, ny), c) for o in range(1, ny)]
    z_peers = [tile_of(lax.rem(z + o, nz), y, c) for o in range(1, nz)]
    far = [(ox, oz) for oz in range(nz) for ox in range(nx) if ox or oz]
    xz_peers = [{"row": lax.rem(x + ox, nx), "tile": (lax.rem(z + oz, nz) * ny + y) * nc + c} for ox, oz in far]
    barrier = pltpu.get_barrier_semaphore()
    peers = [core_peer] + y_peers + xz_peers
    for p in peers:
        pl.semaphore_signal(barrier, inc=1, device_id=p, device_id_type=MESH)
    count = [0]

    def push(src, dst, peer):
        k = count[0]
        count[0] += 1
        copy = pltpu.make_async_remote_copy(
            src_ref=src, dst_ref=dst, send_sem=send.at[k], recv_sem=recv.at[k],
            device_id=peer, device_id_type=MESH)
        copy.start()
        return copy

    def keep(i):
        slot = lax.rem(i, 2)
        return pltpu.make_async_copy(buf.at[slot], cache.at[pl.ds(2 * i, 2)], sem.at[slot])

    panels, width = cache.shape[0], cache.shape[1]

    def step(i, _):
        slot = lax.rem(i, 2)

        @pl.when(i >= 2)
        def _():
            keep(i - 2).wait()

        col = pl.multiple_of(i * 2 * width, 2 * width)
        tb = saug.at[pl.ds(col, 2 * width)]
        for r in range(nx - 1):
            v = values(dot(tb[...], taug[:, r * quarter : (r + 1) * quarter]))
            for s in range(2):
                buf[slot, s, :, r * quarter : (r + 1) * quarter] = v[s * width : (s + 1) * width]
        keep(i).start()
        return 0

    edges = [sum(shares[:k]) for k in range(len(shares) + 1)]

    def work(k):
        if edges[k + 1] > edges[k]:
            lax.fori_loop(edges[k], edges[k + 1], step, 0)

    def finish(made):
        for copy in made:
            copy.wait()

    s1[...] = part[:, :, pl.ds(pl.multiple_of((1 - c) * half, half), half)].astype(BF16)
    pl.semaphore_wait(barrier, len(peers))
    flight = [push(s1, r1, core_peer)]
    work(0)
    finish(flight)
    for q in range(ny):
        at = pl.multiple_of(c * half + q * lanes, lanes)
        a = part[:, :, pl.ds(at, lanes)] + r1[:, :, q * lanes : (q + 1) * lanes].astype(F32)
        a1[q] = a
        s2[q] = a.astype(BF16)
    flight = [push(s2.at[lax.rem(y + o, ny)], r2.at[o - 1], y_peers[o - 1]) for o in range(1, ny)]
    work(1)
    finish(flight)
    for q in range(nz):
        cut = slice(q * kz, (q + 1) * kz)
        a = a1[y, :, cut, :]
        for o in range(1, ny):
            a = a + r2[o - 1, :, cut, :].astype(F32)
        a3[q] = a
        s3[q] = a.astype(BF16)
    flight = [push(s3.at[lax.rem(z + o, nz)], r3.at[o - 1], z_peers[o - 1]) for o in range(1, nz)]
    work(2)
    finish(flight)
    a = a3[z]
    for o in range(1, nz):
        a = a + r3[o - 1].astype(F32)
    low[...] = a.astype(BF16)
    full[c, y, z, x] = low[x]
    flight = [push(low.at[lax.rem(x + ox, nx)], full.at[c, y, z, x], p) for (ox, oz), p in zip(far, xz_peers)]
    work(3)
    finish(flight)
    flight = [push(full.at[c, y], full.at[c, y], p) for p in y_peers]
    near = [push(full.at[c, y], full.at[c, y], core_peer)]
    work(4)
    finish(flight)
    near += [push(full.at[c, lax.rem(y + o, ny)], full.at[c, lax.rem(y + o, ny)], core_peer) for o in range(1, ny)]
    work(5)
    finish(near)
    out[...] = full[...]
    if edges[-1]:
        keep(panels // 2 - 2).wait()
        keep(panels // 2 - 1).wait()


def eliminate(blk, left, right, linv):
    n = left.shape[0]
    at = pl.multiple_of(blk * 8, 8)
    low, inv = left[...], right[...]
    rid = lax.broadcasted_iota(jnp.int32, (n, 1), 0)
    rows, gains = left[pl.ds(at, 8), :], right[pl.ds(at, 8), :]
    r8 = lax.broadcasted_iota(jnp.int32, (8, 1), 0)
    for j in range(8):
        top, gain = rows[j : j + 1], gains[j : j + 1]
        scale = 1.0 / top[:, j : j + 1]
        f8 = jnp.where(r8 > j, rows[:, j : j + 1] * scale, 0.0)
        f = jnp.where(rid >= at + 8, low[:, j : j + 1] * scale, 0.0)
        rows = rows - f8 * top
        gains = gains - f8 * gain
        low = low - f * top
        inv = inv - f * gain
    left[...] = pltpu.roll(low, n - 8, 1)
    right[...] = inv
    lane = lax.broadcasted_iota(jnp.int32, (8, n), 1)
    d = jnp.sum(jnp.where(lane == r8, rows, 0.0), axis=1, keepdims=True)
    linv[pl.ds(at, 8), :] = gains * lax.rsqrt(d)


def dot_full(a, b):
    return jnp.dot(a, b, precision=lax.Precision.HIGHEST, preferred_element_type=F32)


DEPTH = 3


def project_body(flags_hbm, low, own_cache, cache, basis, proj, flags, st, left, right, linv, z, own_buf, buf, fsem, sem):
    panels, width = cache.shape[0], cache.shape[1]
    n = proj.shape[0]
    nc, ny, nz, nx, kz, lanes = low.shape
    quarter = nc * ny * lanes
    steps = panels // 2
    x = lax.axis_index("row")

    def in_copies(i):
        slot = lax.rem(i, DEPTH)
        two = pl.ds(2 * i, 2)
        return [pltpu.make_async_copy(own_cache.at[two], own_buf.at[slot], sem.at[slot, 0]),
                pltpu.make_async_copy(cache.at[two], buf.at[slot], sem.at[slot, 1])]

    flag_copy = pltpu.make_async_copy(flags_hbm, flags, fsem)
    flag_copy.start()
    for i in range(DEPTH - 1):
        for copy in in_copies(i):
            copy.start()
    for k in range(nx):
        q = lax.rem(x + k, nx)
        for c in range(nc):
            for y in range(ny):
                at = k * quarter + (c * ny + y) * lanes
                st[:, at : at + lanes] = low[c, y, :, q].reshape(n, lanes)
    gram = dot_nt(st[...], st[...])
    ri = lax.broadcasted_iota(jnp.int32, (n, n), 0)
    ci = lax.broadcasted_iota(jnp.int32, (n, n), 1)
    eye = (ri == ci).astype(F32)
    shift = 0.0001 * jnp.sum(gram * eye) / n
    left[...] = gram + shift * eye
    right[...] = eye

    def step(i, _):
        slot = lax.rem(i, DEPTH)

        @pl.when(i + DEPTH - 1 < steps)
        def _():
            for copy in in_copies(i + DEPTH - 1):
                copy.start()

        for copy in in_copies(i):
            copy.wait()
        own = own_buf[slot].reshape(2 * width, quarter)
        rest = buf[slot].reshape(2 * width, (nx - 1) * quarter)
        o = dot_nt(st[:, :quarter], own) + dot_nt(st[:, quarter:], rest)
        z[:, pl.ds(pl.multiple_of(i * 2 * width, 2 * width), 2 * width)] = o
        eliminate(i, left, right, linv)
        return 0

    lax.fori_loop(0, steps, step, 0)
    flag_copy.wait()
    factor = linv[...]
    me = lax.axis_index("tile")
    own = basis.shape[0]
    per = quarter // own
    k = lax.rem(me // per - x + nx, nx)
    at = pl.multiple_of(k * quarter + lax.rem(me, per) // 2 * 128, 128)
    block = dot_full(factor, st[:, pl.ds(at, 128)].astype(F32)).T
    basis[...] = jnp.where(lax.rem(me, 2) == 0, block[:own], block[own:])
    for w in range(0, panels, 8):
        o = dot_full(factor, z[:, w * width : (w + 8) * width])
        for g in range(w, w + 8):
            part = o[:, (g - w) * width : (g - w + 1) * width]
            proj[:, g * width : (g + 1) * width] = jnp.where(flags[x, 0, g] > 0, part, 0.0).astype(BF16)


SHARES = (1, 4, 3, 3, 4, 1)


def sum_call(part, tr, sa, shares):
    nx, n, quarter = part.shape
    rest = tr.shape[1]
    cols = sa.shape[0]
    nc, ny = 2, 4
    nz = lax.axis_size("tile") // (nc * ny)
    lanes = quarter // (nc * ny)
    kz = n // nz
    width = 128
    copies = 1 + ny + nz + nx * nz + ny
    vmem = pl.BlockSpec(memory_space=pltpu.VMEM)
    hbm = pl.BlockSpec(memory_space=pltpu.HBM)
    dma = pltpu.SemaphoreType.DMA
    VM = pltpu.VMEM
    return pl.pallas_call(
        functools.partial(sum_body, (nx, nz, ny, nc), shares),
        in_specs=[vmem, vmem, vmem],
        out_specs=[vmem, hbm],
        out_shape=[jax.ShapeDtypeStruct((nc, ny, nz, nx, kz, lanes), BF16),
                   jax.ShapeDtypeStruct((cols // width, width, rest), BF16)],
        scratch_shapes=[
            VM((2, 2, width, rest), BF16),
            VM((nx, n, quarter // nc), BF16), VM((nx, n, quarter // nc), BF16),
            VM((ny, nx, n, lanes), F32), VM((ny, nx, n, lanes), BF16), VM((ny - 1, nx, n, lanes), BF16),
            VM((nz, nx, kz, lanes), BF16), VM((nz, nx, kz, lanes), F32), VM((nz - 1, nx, kz, lanes), BF16),
            VM((nx, kz, lanes), BF16), VM((nc, ny, nz, nx, kz, lanes), BF16),
            dma((copies,)), dma((copies,)), dma((2,))],
        compiler_params=pltpu.CompilerParams(
            collective_id=0, has_side_effects=True, vmem_limit_bytes=48 << 20),
        name="sum_rows",
    )(part, tr, sa)


def local(row_points, source_points, sketch, admissible):
    blocks = lax.axis_size("row")
    panels = admissible.shape[1]
    cols, n = sketch.shape
    width = cols // panels
    rows = row_points.shape[1] // blocks
    quarter = rows // blocks
    tiles = lax.axis_size("tile")
    nc, ny, nx = 2, 4, blocks
    nz = tiles // (nc * ny)
    lanes = quarter // (nc * ny)
    kz = n // nz
    vmem = pl.BlockSpec(memory_space=pltpu.VMEM)
    hbm = pl.BlockSpec(memory_space=pltpu.HBM)
    dma = pltpu.SemaphoreType.DMA
    VM = pltpu.VMEM
    rest = rows - quarter
    flags, ta, tr, sa, skt = pl.pallas_call(
        prepare_body,
        in_specs=[hbm] * 4,
        out_specs=[vmem] * 5,
        out_shape=[jax.ShapeDtypeStruct((blocks, 8, 128), jnp.int32), jax.ShapeDtypeStruct((KA, rows), BF16),
                   jax.ShapeDtypeStruct((KA, rest), BF16), jax.ShapeDtypeStruct((cols, KA), BF16),
                   jax.ShapeDtypeStruct((n, cols), BF16)],
        scratch_shapes=[
            VM((1, panels), jnp.int32),
            VM((3, rows), F32), VM((3, rest), F32), VM((3, cols), F32), VM((cols, n), BF16), VM((KA, max(rows, cols)), F32),
            VM((8, 128), jnp.int32), VM((blocks, 8, 128), jnp.int32), dma((nx - 1,)), dma((nx - 1,)), dma((2 * nx + 2,))],
        compiler_params=pltpu.CompilerParams(
            collective_id=1, has_side_effects=True, vmem_limit_bytes=16384 << 10),
        name="prepare",
    )(*[pltpu.with_memory_space_constraint(v, pltpu.HBM)
        for v in (admissible, row_points, source_points, sketch)])
    part, own_cache = pl.pallas_call(
        sketch_body,
        in_specs=[hbm, vmem, vmem, vmem],
        out_specs=[vmem, hbm],
        out_shape=[jax.ShapeDtypeStruct((blocks, n, quarter), F32),
                   jax.ShapeDtypeStruct((panels, width, quarter), BF16)],
        scratch_shapes=[
            pltpu.SMEM((blocks, 8, 128), jnp.int32),
            pltpu.SMEM((blocks, panels + 1), jnp.int32), pltpu.SMEM((3, blocks * panels // 2 + 5), jnp.int32),
            VM((2, 2 * width, KA), BF16), VM((2, n, 2 * width), BF16), VM((2, n, 2 * width), BF16),
            VM((2 * width, quarter), F32), VM((2 * width, quarter), F32),
            VM((2 * width, quarter), BF16), VM((2 * width, quarter), BF16),
            VM((panels // 2, 2 * width, quarter), BF16), dma, dma((panels // 2, 2))],
        compiler_params=pltpu.CompilerParams(vmem_limit_bytes=49152 << 10),
        name="sketch",
    )(flags, ta, sa, skt)
    low, cache = sum_call(part, tr, sa, SHARES)
    basis, proj = pl.pallas_call(
        project_body,
        in_specs=[hbm, vmem, hbm, hbm],
        out_specs=[vmem, vmem],
        out_shape=[jax.ShapeDtypeStruct((rows // tiles, n), F32), jax.ShapeDtypeStruct((n, cols), BF16)],
        scratch_shapes=[
            pltpu.SMEM((blocks, 8, 128), jnp.int32),
            VM((n, rows), BF16), VM((n, n), F32), VM((n, n), F32), VM((n, n), F32), VM((n, cols), F32),
            VM((DEPTH, 2, width, quarter), BF16), VM((DEPTH, 2, width, rest), BF16), dma, dma((DEPTH, 2))],
        compiler_params=pltpu.CompilerParams(vmem_limit_bytes=48 << 20),
        name="project",
    )(flags, low, own_cache, cache)
    return (basis, proj[None])


def solution(mesh):
    in_specs = (P(), P(None, "tile"), P("tile", None), P("row", "tile"))
    out_specs = (P(("row", "tile"), None), P("row", None, "tile"))
    return jax.shard_map(local, mesh=mesh, in_specs=in_specs, out_specs=out_specs, check_vma=False)
```
